32 devices in a mesh: tbl: 16 (over z, x, core), hst: 2 (over y).
Axes of the slice: x: 2, y: 2, z: 4, core: 2. Of those that a mesh axis runs over, the one named last changes fastest.
Arguments:
- pooled: bfloat16 [8192, 512], P('tbl'), may hold values from -6 to 6
- w_up: bfloat16 [512, 4096], P(None, 'hst'), may hold values from -0.25 to 0.25
- grad_out: bfloat16 [8192, 4096], P('tbl', 'hst'), may hold values from -6 to 6
- owners: int32 [4, 8192, 8], P('hst', 'tbl'), may hold values from 0 to 15, all different within a row; in each aligned block of 512 rows (0 to 511, 512 to 1023, ..., all dimensions but the last counted through in order) at most 512 rows name the same one
- rows: int32 [4, 8192, 8], P('hst', 'tbl'), may hold values from 0 to 1023
- lookup_weight: bfloat16 [4, 8192, 8], P('hst', 'tbl'), may hold values from 0.25 to 2
- lens: int32 [4, 8192], P('hst', 'tbl'), may hold values from 4 to 8
- slot_map: int32 [16, 2, 2048], P('tbl', 'hst'), may hold values from 0 to 2047, each once within a row
- cache_weight: float32 [16, 2, 2048, 128], P('tbl', 'hst'), may hold values from -6 to 6
- cache_accum: float32 [16, 2, 2048], P('tbl', 'hst'), may hold values from 0.1 to 10
- evict_slots: int32 [16, 2, 256], P('tbl', 'hst'), may hold values from 0 to 2047, as said below
- evict_dest: int32 [16, 2, 256], P('tbl', 'hst'), may hold values from 0 to 1, as said below
- evict_count: int32 [16, 2], P('tbl', 'hst'), may hold values from 128 to 256
Outputs:
- grad_up: float32 [512, 4096], P('tbl', 'hst')
- new_weight: float32 [16, 2, 2048, 128], P('tbl', 'hst')
- new_accum: float32 [16, 2, 2048], P('tbl', 'hst')
- held_rows: float32 [16, 2, 2, 128, 128], P('tbl', 'hst')
- held_accum: float32 [16, 2, 2, 128], P('tbl', 'hst')
The draws below stay inside these ranges and needn't reach their ends.
Inputs may be any that keep to these rules, and one draw needn't show every extreme that they name: The 8 owners of one bag differ. Among the 512 samples of one index of tbl and one table, no owner is named by more than 512 lookup positions, used or not; some owner is named by exactly 512 in some such block. `evict_slots`: the 256 slots of one device's list differ. `evict_dest`: among the used entries of one device, no holder appears more than 128 times, and one holder appears exactly 128 times.
All inputs are finite; a program needn't handle non-finite values.
Results may differ from the reference program's by a relative error of at most 0.0029.
Values may be sent and summed in bfloat16 or wider, within the bound.
A program may use at most 64 MiB of HBM per device.

```python
import math
import jax
import jax.numpy as jnp
import numpy as np
from jax import lax

EMB = 128
HIDDEN_SIZE = 4096
TABLES_DEV = 2
BAG = 8
B_DEV = 512
ROWS_DEV = 1024
EVICT = 256
OWNERS = 16
HOLDERS = 2
B = 8192
TABLES = 4
FEAT = 512
SLOTS = 2048
CAP = 128
MOST = 512


def eviction_plan(key):
    keys = jax.random.split(jax.random.fold_in(key, 7), 4)
    devices = OWNERS * HOLDERS
    amounts = jax.random.randint(keys[0], (devices,), CAP, EVICT + 1)
    favored = jax.random.randint(keys[1], (devices,), 0, HOLDERS)
    offsets = jax.random.randint(keys[2], (devices, EVICT), 1, HOLDERS)
    positions = jnp.arange(EVICT, dtype=jnp.int32)
    baseline = jnp.where(positions[None, :] < CAP, favored[:, None], (favored[:, None] + offsets) % HOLDERS)
    scores = jax.random.randint(keys[3], (devices, EVICT), 0, 1 << 20)
    sorting = jnp.where(positions[None, :] < amounts[:, None], scores * EVICT + positions[None, :], (1 << 30) + positions[None, :])
    arrange = jnp.argsort(sorting, axis=1, stable=True)
    targets = jnp.take_along_axis(baseline, arrange, axis=1)
    return (targets.reshape(OWNERS, HOLDERS, EVICT).astype(jnp.int32), amounts.reshape(OWNERS, HOLDERS).astype(jnp.int32))


def draw_evict_dest(key, part):
    return eviction_plan(key)[0]


def draw_evict_count(key, part):
    return eviction_plan(key)[1]


def draw_evict_slots(key, part):
    keys = jax.random.split(jax.random.fold_in(key, 11), OWNERS * HOLDERS)
    chosen = jax.vmap(lambda single: jax.random.permutation(single, SLOTS)[:EVICT])(keys)
    return chosen.reshape(OWNERS, HOLDERS, EVICT).astype(jnp.int32)


def plant(array, own_key, low, top_value):
    extent = array.shape
    spot = [jax.random.randint(jax.random.fold_in(own_key, axis), (), 0, extent[axis]) for axis in range(len(extent))]
    array = array.at[tuple(spot)].set(low)
    longest = extent.index(max(extent))
    spot[longest] = (spot[longest] + 1) % extent[longest]
    return array.at[tuple(spot)].set(top_value)


def strengthened(entries, own_key, source, target, blocks, factor):
    def block_of(position):
        return (jnp.arange(entries.shape[position]) // (entries.shape[position] // blocks)).reshape((-1,) + (1,) * (entries.ndim - 1 - position))

    near = jax.random.permutation(own_key, blocks)[block_of(target)]
    second = (block_of(target) + blocks // 2) % blocks
    return jnp.where((block_of(source) == near) | (block_of(source) == second), factor * entries, entries)


def steps_of(stream_key, shape, cuts, smallest, top_value):
    factor_of = 1.0
    for axis_at, blocks in cuts:
        steps = jax.random.uniform(jax.random.fold_in(jax.random.fold_in(stream_key, 6), axis_at), (blocks,), jnp.float32, smallest / len(cuts), top_value / len(cuts))
        factor_of = factor_of * jnp.repeat(jnp.exp(steps), shape[axis_at] // blocks).reshape((-1,) + (1,) * (len(shape) - 1 - axis_at))
    return factor_of


def assign_block(rng, own, number, rows, amount, top, bound, skew):
    sequence = jax.random.permutation(rng, amount)
    heavy_load, usual = shares(amount, rows * top, bound, skew, True), shares(amount, rows * top, bound, skew, False)
    places = jnp.arange(amount)

    def named(lengths, rotation):
        used = int((lengths > 0).sum())
        fixed = max(1, used // 4)
        passed = fixed + (places - fixed + rotation * (used - fixed)) % max(1, amount - fixed)
        return jnp.zeros((amount,), jnp.int32).at[sequence[jnp.where(places < fixed, places, passed)]].set(jnp.asarray(lengths, jnp.int32))

    lengths = jnp.where(number % 4 == 0, named(heavy_load, number // 4), named(usual, number - number // 4 - 1))
    mixed = jax.random.permutation(jax.random.fold_in(own, 3), amount)
    giver, receiver = mixed[0:amount // 2 * 2:2], mixed[1:amount // 2 * 2:2]
    slack = jnp.minimum(lengths[giver] - 1, bound - lengths[receiver]) // 2
    slack = jnp.where((giver == sequence[0]) | (receiver == sequence[0]) | (lengths[receiver] == 0), 0, jnp.maximum(slack, 0))
    passed = jax.random.randint(jax.random.fold_in(own, 4), (amount // 2,), 0, 1 << 20) % (slack + 1)
    lengths = lengths.at[giver].add(-passed).at[receiver].add(passed)
    members = jnp.searchsorted(jnp.cumsum(lengths), jnp.arange(rows * top), side="right").astype(jnp.int32)
    grid = members.reshape(top, rows).T
    grid = grid[jax.random.permutation(jax.random.fold_in(own, 1), rows)]
    rotation = jax.random.randint(jax.random.fold_in(own, 2), (rows, 1), 0, top)
    return jnp.take_along_axis(grid, (jnp.arange(top)[None, :] + rotation) % top, axis=1)


def shares(number_of, total, bound, slope, full):
    portions = [(1 << 20) // math.isqrt(rank ** slope) + 1 for rank in range(1, number_of + 1)]
    largest = bound if full else min(bound, max(-(-total // number_of), total * portions[0] // sum(portions)))
    least = 1 if total - largest >= number_of - 1 else 0
    given, rest = [largest] + [least] * (number_of - 1), total - largest - least * (number_of - 1)
    while rest > 0:
        candidates = [i for i in range(1, number_of) if given[i] < largest] or [i for i in range(1, number_of) if given[i] < bound]
        mass, budget = sum([portions[i] for i in candidates]), rest
        for i in candidates:
            extra = min(bound - given[i], max(1, budget * portions[i] // mass), rest)
            given[i] = given[i] + extra
            rest = rest - extra
    return np.array(given)


def gaussian(key, extent, scale, bound, cuts=(), held_as=jnp.bfloat16):
    values = scale * jax.random.normal(key, extent, jnp.float32)
    if cuts:
        values = values * steps_of(key, extent, cuts, -0.22, 0.18)
    return jnp.clip(values, -bound, bound).astype(held_as)


def bell_draw_with(key, extent, width, limit, cuts, heavy, held_as=jnp.bfloat16):
    result = width * jax.random.normal(key, extent, jnp.float32)
    if cuts:
        result = result * steps_of(key, extent, cuts, -0.22, 0.18)
    return jnp.clip(strengthened(result, jax.random.fold_in(key, 3), *heavy), -limit, limit).astype(held_as)


def setup_inputs(seed: int = 0) -> dict:
    streams_of = jax.random.split(jax.random.key(seed), 14)
    pooled = bell_draw_with(streams_of[0], (B, FEAT), 1.0, 6.0, ((0, 16),), (0, 1, 16, 2.0))
    w_up = gaussian(streams_of[1], (FEAT, HIDDEN_SIZE), FEAT ** -0.5, 0.25, ((1, 2),))
    grad_out = gaussian(streams_of[2], (B, HIDDEN_SIZE), 1.0, 6.0, ((0, 16), (1, 2)))
    owners_keys = jax.random.split(jax.random.fold_in(streams_of[3], 1), TABLES * B // B_DEV)
    owners_turns = jax.random.permutation(jax.random.fold_in(streams_of[3], 3), TABLES * B // B_DEV)
    owners = jax.vmap(lambda own, number: assign_block(jax.random.fold_in(streams_of[3], 2), own, number, B_DEV, OWNERS, BAG, MOST, 1))(owners_keys, owners_turns).reshape((TABLES, B, BAG))
    rows = plant(jax.random.randint(streams_of[4], (TABLES, B, BAG), 0, ROWS_DEV), jax.random.fold_in(streams_of[4], 1), 0, ROWS_DEV - 1).astype(jnp.int32)
    lookup_weight = jnp.clip(jnp.exp(math.log(2.0) - 2.0794415 * jax.random.uniform(streams_of[5], (TABLES, B, BAG), jnp.float32) ** steps_of(streams_of[5], (TABLES, B, BAG), ((0, 2), (1, 16)), -0.2, 0.2)), 0.25, 2.0).astype(jnp.bfloat16)
    lens = plant(jax.random.randint(streams_of[6], (TABLES, B), (BAG + 1) // 2, BAG + 1), jax.random.fold_in(streams_of[6], 1), (BAG + 1) // 2, BAG).astype(jnp.int32)
    slot_map = jax.vmap(lambda own: jax.random.permutation(own, SLOTS))(jax.random.split(streams_of[7], OWNERS * HOLDERS)).reshape((OWNERS, HOLDERS, SLOTS)).astype(jnp.int32)
    cache_weight = gaussian(streams_of[8], (OWNERS, HOLDERS, SLOTS, EMB), 1.0, 6.0, ((0, 16), (1, 2)), jnp.float32)
    cache_accum = jnp.clip(jnp.exp(math.log(10.0) - 4.6051702 * jax.random.uniform(streams_of[9], (OWNERS, HOLDERS, SLOTS), jnp.float32) ** steps_of(streams_of[9], (OWNERS, HOLDERS, SLOTS), ((0, 16), (1, 2)), -0.2, 0.2)), 0.1, 10.0)
    evict_slots = draw_evict_slots(jax.random.fold_in(streams_of[13], 71), 0)
    evict_dest = draw_evict_dest(jax.random.fold_in(streams_of[13], 71), 0)
    evict_count = draw_evict_count(jax.random.fold_in(streams_of[13], 71), 0)
    return {"pooled": pooled, "w_up": w_up, "grad_out": grad_out, "owners": owners, "rows": rows, "lookup_weight": lookup_weight, "lens": lens, "slot_map": slot_map, "cache_weight": cache_weight, "cache_accum": cache_accum, "evict_slots": evict_slots, "evict_dest": evict_dest, "evict_count": evict_count}


LEARN_RATE = 0.05
EPSILON = 1e-08

def reference(pooled, w_up, grad_out, owners, rows, lookup_weight, lens, slot_map, cache_weight, cache_accum, evict_slots, evict_dest, evict_count):
    preact = jnp.dot(pooled, w_up, preferred_element_type=jnp.float32)
    sigmoid_z = jax.nn.sigmoid(preact)
    delta = (grad_out.astype(jnp.float32) * sigmoid_z * (1.0 + preact * (1.0 - sigmoid_z))).astype(jnp.bfloat16)
    grad_up = lax.dot_general(pooled, delta, (((0,), (0,)), ((), ())), preferred_element_type=jnp.float32)
    feature_grad = lax.dot_general(delta, w_up, (((1,), (1,)), ((), ())), preferred_element_type=jnp.float32)
    bag_grad = feature_grad.astype(jnp.bfloat16).reshape(B, TABLES, EMB)
    bag_major = jnp.transpose(bag_grad, (1, 0, 2)).astype(jnp.float32)
    positions = jnp.arange(BAG, dtype=jnp.int32)
    used = positions[None, None, :] < lens[:, :, None]
    flat_size = OWNERS * HOLDERS * SLOTS

    def one_table(running, table):
        group = table // TABLES_DEV
        local_table = table % TABLES_DEV
        own_rows = owners[table]
        slot_index = slot_map[own_rows, group, local_table * ROWS_DEV + rows[table]]
        flat_index = (own_rows * HOLDERS + group) * SLOTS + slot_index
        flat_index = jnp.where(used[table], flat_index, flat_size).astype(jnp.int32)
        scaled = (lookup_weight[table].astype(jnp.float32)[:, :, None] * bag_major[table][:, None, :]).astype(jnp.bfloat16)
        scaled = lax.optimization_barrier(scaled).astype(jnp.float32)
        running = running.at[flat_index.reshape(-1)].add(scaled.reshape(-1, EMB), mode='drop')
        return (running, None)
    slot_grad, _ = lax.scan(one_table, jnp.zeros((flat_size, EMB), jnp.float32), jnp.arange(TABLES, dtype=jnp.int32))
    slot_grad = slot_grad.reshape(OWNERS, HOLDERS, SLOTS, EMB)
    new_accum = cache_accum + lax.optimization_barrier(jnp.mean(slot_grad * slot_grad, axis=-1))
    new_weight = cache_weight - LEARN_RATE * slot_grad / (jnp.sqrt(new_accum)[..., None] + EPSILON)
    leaving = jnp.take_along_axis(new_weight, evict_slots[..., None], axis=2)
    leaving_accum = jnp.take_along_axis(new_accum, evict_slots, axis=2)
    live = jnp.arange(EVICT, dtype=jnp.int32)[None, None, :] < evict_count[:, :, None]
    picks = ((evict_dest[..., None] == jnp.arange(HOLDERS, dtype=jnp.int32)) & live[..., None]).astype(jnp.int32)
    placed = lax.optimization_barrier(jnp.sum((jnp.cumsum(picks, axis=2) - 1) * picks, axis=-1))
    device_index = jnp.arange(OWNERS, dtype=jnp.int32)[:, None] * HOLDERS + jnp.arange(HOLDERS, dtype=jnp.int32)[None, :]
    goal = device_index[:, :, None] * (HOLDERS * CAP) + evict_dest * CAP + placed
    goal = jnp.where(live, goal, OWNERS * HOLDERS * HOLDERS * CAP).astype(jnp.int32)
    held_flat = jnp.zeros((OWNERS * HOLDERS * HOLDERS * CAP, EMB), jnp.float32).at[goal.reshape(-1)].set(leaving.reshape(-1, EMB), mode='drop')
    accum_flat = jnp.zeros((OWNERS * HOLDERS * HOLDERS * CAP,), jnp.float32).at[goal.reshape(-1)].set(leaving_accum.reshape(-1), mode='drop')
    held_rows = jnp.transpose(held_flat.reshape(OWNERS, HOLDERS, HOLDERS, CAP, EMB), (0, 2, 1, 3, 4))
    held_accum = jnp.transpose(accum_flat.reshape(OWNERS, HOLDERS, HOLDERS, CAP), (0, 2, 1, 3))
    return (grad_up, new_weight, new_accum, held_rows, held_accum)
```

```python
import functools

import jax
import jax.numpy as jnp
from jax import lax
from jax.experimental import pallas as pl
from jax.experimental.pallas import tpu as pltpu
from jax.sharding import PartitionSpec as P

LEARN_RATE = 0.05
EPSILON = 1e-08
MESH = pl.DeviceIdType.MESH
BLOCKS = 2
SUBS = 2
PIECES = BLOCKS * SUBS
CUTS = 4
RADIX = 256
ROW_STEP = 2048.0
WEIGHT_STEP = 512.0
F32 = jnp.float32
BF16 = jnp.bfloat16
NT_DIMS = (((1,), (1,)), ((), ()))


def iota(shape, axis):
    return lax.broadcasted_iota(jnp.int32, shape, axis)


def step_kernel(
    nz, nx, nh, tables, rows_dev, tile,
    pooled, w_up, grad_out, owners, rows, lookup_weight, lens, slot_map,
    weight, accum, evict_slots, evict_dest, evict_count,
    grad_up, new_weight, new_accum, held_rows, held_accum,
    pooled_v, pooled_t, w_v, go_v, delta, own_v, row_v, lw_v, len_v, map_v, weight_v, accum_v,
    es_v, ed_v, ec_v,
    fown, fsend, ybuf, gat, idx, idxb, grad, rcore, chain, rin, lin, xs, xr, place,
    wide, inv_v, src_v, inv_s, src_s, ev_w, ev_a, ev_g, ev_rows, ev_acc, rows_in, acc_in,
    ld_s, sm_s, y_s, y_r, i_s, i_r, azr_s, azl_s, ax_s, ac_s, g_r, rc_s, rc_r,
    ch_s, rin_r, lin_r, xs_s, xr_r, er_s, er_r, ea_s, ea_r,
):
    n = nz * nx * 2
    me = lax.axis_index("tbl")
    h = lax.axis_index("hst")
    c = lax.rem(me, 2)
    zx = me // 2
    x = lax.rem(zx, nx)
    z = zx // nx
    other = 1 - c
    batch, hid = grad_out.shape
    feat_n = pooled.shape[1]
    width = ybuf.shape[-1]
    emb = width // tables
    bag = owners.shape[1]
    slots = weight.shape[0]
    list_len = evict_slots.shape[1]
    cap = ev_rows.shape[1]
    out_rows = grad.shape[4]
    cut = hid // CUTS
    piece = batch // PIECES
    block = batch // BLOCKS
    tiles = hid // tile

    def at(zi, xi, ci):
        return (zi * nx + xi) * 2 + ci

    def xof(d):
        return lax.rem(x + d, nx)

    def rcopy(src, dst, s, r, dev):
        return pltpu.make_async_remote_copy(
            src_ref=src, dst_ref=dst, send_sem=s, recv_sem=r,
            device_id=dev, device_id_type=MESH,
        )

    def cols(hh):
        return pl.ds(pl.multiple_of(hh * width, width), width)

    def span(k):
        return pl.ds(k * piece, piece)

    def spanb(k):
        return pl.ds(k * block, block)

    def cutcols(j):
        return pl.ds(j * cut, cut)

    loads = [pltpu.make_async_copy(pooled, pooled_v, ld_s.at[0])]
    w_loads = [
        pltpu.make_async_copy(
            w_up.at[:, pl.ds(j * tile, tile)], w_v.at[:, pl.ds(j * tile, tile)], ld_s.at[1 + j]
        )
        for j in range(tiles)
    ]
    g_loads = [
        pltpu.make_async_copy(grad_out.at[spanb(k)], go_v.at[spanb(k)], ld_s.at[1 + tiles + k])
        for k in range(BLOCKS)
    ]
    base = 1 + tiles + BLOCKS
    small = [
        pltpu.make_async_copy(src, dst, ld_s.at[base + k])
        for k, (src, dst) in enumerate((
            (owners, own_v), (rows, row_v), (lookup_weight, lw_v), (lens, len_v),
            (slot_map, map_v), (evict_slots, es_v), (evict_dest, ed_v), (evict_count, ec_v),
            (accum, accum_v), (weight, weight_v),
        ))
    ]
    loads[0].start()
    w_loads[0].start()
    g_loads[0].start()
    for copy in w_loads[1:] + g_loads[1:] + small:
        copy.start()

    barrier = pltpu.get_barrier_semaphore()

    def greet(d, carry):
        pl.semaphore_signal(
            barrier, inc=1, device_id={"tbl": lax.rem(me + d, n)}, device_id_type=MESH
        )
        return carry

    lax.fori_loop(1, n, greet, 0)
    for d in range(1, nh):
        pl.semaphore_signal(
            barrier, inc=1, device_id={"hst": lax.rem(h + d, nh)}, device_id_type=MESH
        )

    def y_copy(d, k):
        h2 = lax.rem(h + d, nh)
        return rcopy(
            fsend.at[d - 1, span(k)], ybuf.at[h, span(k)], y_s.at[d, k], y_r.at[h, k], {"hst": h2}
        )

    def y_arrival(d, k):
        h2 = lax.rem(h + d, nh)
        return rcopy(
            fsend.at[d - 1, span(k)], ybuf.at[h2, span(k)], y_s.at[d, k], y_r.at[h2, k],
            {"hst": h2},
        )

    def deltas(k):
        g_loads[k].wait()
        for j in range(tiles):
            if k == 0:
                w_loads[j].wait()
            cs = pl.ds(j * tile, tile)
            p = jnp.dot(pooled_v[spanb(k), :], w_v[:, cs], preferred_element_type=F32)
            s = jax.nn.sigmoid(p)
            g = go_v[spanb(k), cs].astype(F32)
            delta[spanb(k), cs] = (g * s * (1.0 + p * (1.0 - s))).astype(BF16)

    def feats(k):
        for d in range(1, nh):
            h2 = lax.rem(h + d, nh)
            part = lax.dot_general(
                delta[spanb(k), :], w_v[cols(h2), :], NT_DIMS, preferred_element_type=F32
            )
            fsend[d - 1, spanb(k)] = part.astype(BF16)
            for q in range(SUBS):
                y_copy(d, k * SUBS + q).start()
        fown[spanb(k), :] = lax.dot_general(
            delta[spanb(k), :], w_v[cols(h), :], NT_DIMS, preferred_element_type=F32
        )

    loads[0].wait()
    deltas(0)
    pl.semaphore_wait(barrier, n - 1 + nh - 1)
    feats(0)
    deltas(1)
    feats(1)

    def g_copy(slot, k, sem, dev):
        ref = gat.at[slot, span(k)]
        return rcopy(ref, ref, sem, g_r.at[slot, k], {"tbl": dev})

    def right_copy(zi, k):
        return g_copy(at(zi, x, c), k, azr_s.at[zi, k], at(z + 1, x, c))

    def left_copy(zi, k):
        return g_copy(at(zi, x, c), k, azl_s.at[zi, k], at(z - 1, x, c))

    def x_copy(zi, d, k):
        return g_copy(at(zi, x, c), k, ax_s.at[zi, d, k], at(z, xof(d), c))

    def c_copy(zi, xi, k):
        return g_copy(at(zi, xi, c), k, ac_s.at[zi, xi, k], at(z, x, other))

    def arrived(slot, k):
        g_copy(slot, k, ac_s.at[0, 0, k], at(z, x, other)).wait_recv()

    def gather_start(k):
        total = fown[span(k), :]
        for d in range(1, nh):
            y_arrival(d, k).wait_recv()
            total = total + ybuf[lax.rem(h + d, nh), span(k)].astype(F32)
        gat[me, span(k)] = total.astype(BF16)

        @pl.when(z + 1 < nz)
        def _():
            right_copy(z, k).start()

        @pl.when(z >= 1)
        def _():
            left_copy(z, k).start()

        for d in range(1, nx):
            x_copy(z, d, k).start()
        c_copy(z, x, k).start()

    def core_copy(j):
        return rcopy(
            grad.at[j, :, :, other], rcore.at[j], rc_s.at[j], rc_r.at[j], {"tbl": at(z, x, other)}
        )

    def weight_grad(j):
        part = jnp.dot(pooled_t[...], delta[:, cutcols(j)], preferred_element_type=F32)
        grad[j] = part.reshape(nz, nx, 2, out_rows, cut)
        core_copy(j).start()

    def i_copy(d):
        o = lax.rem(me + d, n)
        return rcopy(idx.at[o], idxb.at[me], i_s.at[d], i_r.at[me], {"tbl": o})

    def i_arrival(slot):
        return rcopy(idx.at[slot], idxb.at[slot], i_s.at[0], i_r.at[slot], {"tbl": at(z, x, other)})

    for copy in small:
        copy.wait()
    for t in range(tables):
        used = iota((bag, batch), 0) < len_v[t : t + 1, :]
        code = (row_v[t] + 1).astype(F32) * ROW_STEP + lw_v[t].astype(F32) * WEIGHT_STEP
        code = jnp.where(used, code, 0.0)
        for o in range(n):
            idx[o, t : t + 1, :] = jnp.sum(
                jnp.where(own_v[t] == o, code, 0.0), axis=0, keepdims=True
            )
    idxb[me] = idx[me]

    def i_start(d, carry):
        i_copy(d).start()
        return carry

    lax.fori_loop(1, n, i_start, 0)
    pooled_t[...] = pooled_v[...].T

    for k in range(PIECES):
        gather_start(k)
        for j in range(k * CUTS // PIECES, (k + 1) * CUTS // PIECES):
            weight_grad(j)

    place[...] = jnp.zeros_like(place)
    chunk = min(RADIX, rows_dev)

    def proc(slot):
        codes = idxb[slot]
        bags = gat[slot]
        for t in range(tables):
            code = codes[t : t + 1, :]
            row1 = jnp.floor(code * (1.0 / ROW_STEP))
            wgt = (code - row1 * ROW_STEP) * (1.0 / WEIGHT_STEP)
            row = row1 - 1.0
            part = bags[:, t * emb : (t + 1) * emb]
            for r0 in range(0, rows_dev, chunk):
                ids = iota((chunk, batch), 0).astype(F32) + float(r0)
                mark = jnp.where(ids == row, wgt, 0.0).astype(BF16)
                place[pl.ds(t * rows_dev + r0, chunk), :] += jnp.dot(
                    mark, part, preferred_element_type=F32
                )

    proc(me)

    eye = iota((emb, emb), 0) == iota((emb, emb), 1)
    groups = slots // emb

    def widen(i, carry):
        col = jnp.sum(jnp.where(eye, accum_v[pl.ds(i, 1), :], 0.0), axis=1, keepdims=True)
        wide[pl.ds(i * emb, emb), :] = jnp.broadcast_to(col, (emb, emb))
        return carry

    lax.fori_loop(0, groups, widen, 0)
    home = map_v[...].astype(F32)
    high = jnp.floor(home * (1.0 / emb))
    low = home - high * emb
    from_row = iota((1, slots), 1).astype(F32)
    from_high = jnp.floor(from_row * (1.0 / RADIX))
    from_low = from_row - from_high * RADIX
    in_group = iota((groups, slots), 0).astype(F32) == high
    left = jnp.concatenate(
        [jnp.where(in_group, from_high, 0.0), jnp.where(in_group, from_low, 0.0)], axis=0
    ).astype(BF16)
    right = jnp.where(iota((emb, slots), 0).astype(F32) == low, 1.0, 0.0).astype(BF16)
    found = lax.dot_general(left, right, NT_DIMS, preferred_element_type=F32)
    inv = (found[:groups] * RADIX + found[groups:]).astype(jnp.int32)
    inv_v[...] = jnp.clip(inv, 0, slots - 1)
    inv_copy = pltpu.make_async_copy(inv_v, inv_s, sm_s.at[0])
    inv_copy.start()

    live = iota((1, list_len), 1) < ec_v[...]
    lanes = 8 * -(-nh // 8)
    mine = jnp.where((iota((lanes, list_len), 0) == ed_v[...]) & live, 1.0, 0.0)
    before = jnp.where(iota((list_len, list_len), 0) < iota((list_len, list_len), 1), 1.0, 0.0)
    goal = jnp.dot(mine.astype(BF16), before.astype(BF16), preferred_element_type=F32)
    slot1 = es_v[...].astype(F32) + 1.0
    slot_high = jnp.floor(slot1 * (1.0 / RADIX))
    slot_low = slot1 - slot_high * RADIX
    parts = jnp.where(iota((8, list_len), 0) == 0, slot_high, slot_low).astype(BF16)
    for d in range(nh):
        hot = jnp.where(
            iota((cap, list_len), 0).astype(F32) == goal[d : d + 1], mine[d : d + 1], 0.0
        ).astype(BF16)
        got = lax.dot_general(parts, hot, NT_DIMS, preferred_element_type=F32)
        src = (got[0:1] * RADIX + got[1:2]).astype(jnp.int32)
        src_v[d : d + 1, :] = jnp.clip(src, 0, slots)
    src_copy = pltpu.make_async_copy(src_v, src_s, sm_s.at[1])
    src_copy.start()
    inv_copy.wait()
    src_copy.wait()

    def slot_of(k, p):
        s1 = src_s[k, p]
        return s1 > 0, jnp.maximum(s1 - 1, 0)

    def ev_fetch(i, carry):
        k = i // (cap // 8)
        p = lax.rem(i, cap // 8) * 8
        for q in range(8):
            ok, s = slot_of(k, p + q)
            ev_w[k, pl.ds(p + q, 1), :] = jnp.where(ok, weight_v[pl.ds(s, 1), :], 0.0)
            ev_a[k, pl.ds(p + q, 1), :] = jnp.where(ok, wide[pl.ds(s, 1), :], 0.0)
        return carry

    lax.fori_loop(0, nh * cap // 8, ev_fetch, 0)

    def rin_copy(t, j):
        return rcopy(
            chain.at[t, j], rin.at[t, j], ch_s.at[t, j], rin_r.at[t, j], {"tbl": at(z + 1, x, c)}
        )

    def lin_copy(t, j):
        return rcopy(
            chain.at[t, j], lin.at[t, j], ch_s.at[t, j], lin_r.at[t, j], {"tbl": at(z - 1, x, c)}
        )

    def own_sum(t, j, xi):
        return grad[j, t, xi, c] + rcore[j, t, xi]

    def chain_step(t, j, buf, copy):
        for xi in range(nx):
            s = own_sum(t, j, xi)
            if buf is not None:
                s = s + buf[t, j, xi].astype(F32)
            chain[t, j, xi] = s.astype(BF16)
        copy(t, j).start()

    for j in range(CUTS):
        core_copy(j).wait_recv()

    @pl.when(z == 0)
    def _():
        def body(i, carry):
            for j in range(CUTS):
                chain_step(nz - 1 - i, j, None, rin_copy)
            return carry

        lax.fori_loop(0, nz - 1, body, 0)

    @pl.when(z == nz - 1)
    def _():
        def body(i, carry):
            for j in range(CUTS):
                chain_step(i, j, None, lin_copy)
            return carry

        lax.fori_loop(0, nz - 1, body, 0)

    def from_z(zi, open_end, onward):
        slot = at(zi, x, c)
        for k in range(PIECES):
            arrived(slot, k)

            @pl.when(open_end)
            def _(k=k):
                onward(zi, k).start()

            for dx in range(1, nx):
                x_copy(zi, dx, k).start()
            c_copy(zi, x, k).start()

    def own_proc(slot):
        i_arrival(slot).wait_recv()
        proc(slot)

    def from_x(zi):
        for dx in range(1, nx):
            slot = at(zi, xof(dx), c)
            for k in range(PIECES):
                arrived(slot, k)
                c_copy(zi, xof(dx), k).start()
            own_proc(slot)

    def from_core(zi, xi):
        slot = at(zi, xi, other)
        for k in range(PIECES):
            arrived(slot, k)
        own_proc(slot)

    def from_core_x(zi):
        for dx in range(1, nx):
            from_core(zi, xof(dx))

    zr = nz - 1 - z

    def line_body(j, carry):
        below, above = z - j >= 0, z + j < nz

        @pl.when(below)
        def _():
            from_z(z - j, z + 1 < nz, right_copy)

        @pl.when(above)
        def _():
            from_z(z + j, z >= 1, left_copy)

        s = j - 1

        @pl.when((s <= nz - 2) & (z >= 1) & (z <= s))
        def _():
            t = nz - 1 - s + z
            for q in range(CUTS):
                rin_copy(t, q).wait_recv()
                chain_step(t, q, rin, rin_copy)

        @pl.when((s <= nz - 2) & (zr >= 1) & (zr <= s))
        def _():
            t = s - zr
            for q in range(CUTS):
                lin_copy(t, q).wait_recv()
                chain_step(t, q, lin, lin_copy)

        @pl.when(below)
        def _():
            own_proc(at(z - j, x, c))

        @pl.when(above)
        def _():
            own_proc(at(z + j, x, c))

        @pl.when(z - s >= 0)
        def _():
            from_x(z - s)
            from_core(z - s, x)

        @pl.when((s >= 1) & (z + s < nz))
        def _():
            from_x(z + s)
            from_core(z + s, x)

        @pl.when((s >= 1) & (z - s + 1 >= 0))
        def _():
            from_core_x(z - s + 1)

        @pl.when((s >= 2) & (z + s - 1 < nz))
        def _():
            from_core_x(z + s - 1)

        return carry

    lax.fori_loop(1, nz + 1, line_body, 0)

    def xs_copy(d, j):
        x2 = xof(d)
        return rcopy(xs.at[d - 1, j], xr.at[x, j], xs_s.at[d, j], xr_r.at[x, j], {"tbl": at(z, x2, c)})

    def xs_arrival(d, j):
        x2 = xof(d)
        return rcopy(xs.at[d - 1, j], xr.at[x2, j], xs_s.at[d, j], xr_r.at[x2, j], {"tbl": at(z, x2, c)})

    @pl.when(z >= 1)
    def _():
        for j in range(CUTS):
            rin_copy(z, j).wait_recv()
            for xi in range(nx):
                grad[j, z, xi, c] += rin[z, j, xi].astype(F32)

    @pl.when(z + 1 < nz)
    def _():
        for j in range(CUTS):
            lin_copy(z, j).wait_recv()
            for xi in range(nx):
                grad[j, z, xi, c] += lin[z, j, xi].astype(F32)

    for j in range(CUTS):
        for d in range(1, nx):
            xs[d - 1, j] = own_sum(z, j, xof(d)).astype(BF16)
            xs_copy(d, j).start()

    @pl.when(z == 0)
    def _():
        from_core_x(nz - 1)

    @pl.when(z == nz - 1)
    def _():
        from_core_x(0)

    def gathered(first):
        picks = []
        for q in range(8):
            picks.append(place[pl.ds(first(q), 1), :])
        return jnp.concatenate(picks, axis=0)

    def row_of(s):
        return inv_s[s // emb, lax.rem(s, emb)]

    def ev_gather(i, carry):
        k = i // (cap // 8)
        p = lax.rem(i, cap // 8) * 8
        for q in range(8):
            ok, s = slot_of(k, p + q)
            ev_g[k, pl.ds(p + q, 1), :] = jnp.where(ok, place[pl.ds(row_of(s), 1), :], 0.0)
        return carry

    lax.fori_loop(0, nh * cap // 8, ev_gather, 0)

    def er_copy(d, slot):
        k = lax.rem(h + d, nh)
        return rcopy(ev_rows.at[k], rows_in.at[slot], er_s.at[d], er_r.at[slot], {"hst": k})

    def ea_copy(d, slot):
        k = lax.rem(h + d, nh)
        return rcopy(ev_acc.at[k], acc_in.at[slot], ea_s.at[d], ea_r.at[slot], {"hst": k})

    for d in range(1, nh + 1):
        k = lax.rem(h + d, nh)
        for r0 in range(0, cap, emb):
            span_k = pl.ds(r0, emb)
            g = ev_g[k, span_k]
            acc = ev_a[k, span_k] + jnp.mean(g * g, axis=1, keepdims=True)
            ev_rows[k, span_k] = ev_w[k, span_k] - LEARN_RATE * g / (jnp.sqrt(acc) + EPSILON)
            ev_acc[k, :, span_k] = jnp.sum(jnp.where(eye, acc, 0.0), axis=0, keepdims=True)
        if d < nh:
            er_copy(d, h).start()
            ea_copy(d, h).start()
    held_rows[h] = ev_rows[h]
    held_accum[h] = ev_acc[h]

    def update(i, carry):
        total = jnp.zeros((8, emb), F32)
        for b in range(emb // 8):
            rows_b = pl.ds(pl.multiple_of(i * emb + b * 8, 8), 8)
            g = gathered(lambda q: inv_s[i, b * 8 + q])
            acc = wide[rows_b, :] + jnp.mean(g * g, axis=1, keepdims=True)
            new_weight[rows_b, :] = weight_v[rows_b, :] - LEARN_RATE * g / (
                jnp.sqrt(acc) + EPSILON
            )
            diag = iota((8, emb), 1) == iota((8, emb), 0) + b * 8
            total = total + jnp.where(diag, acc, 0.0)
        new_accum[pl.ds(i, 1), :] = jnp.sum(total, axis=0, keepdims=True)
        return carry

    lax.fori_loop(0, groups, update, 0)

    for j in range(CUTS):
        s = own_sum(z, j, x)
        for d in range(1, nx):
            xs_arrival(d, j).wait_recv()
            s = s + xr[xof(d), j].astype(F32)
        grad_up[:, cutcols(j)] = s

    for d in range(1, nh):
        k = lax.rem(h + d, nh)
        er_copy(d, k).wait_recv()
        ea_copy(d, k).wait_recv()
        held_rows[k] = rows_in[k]
        held_accum[k] = acc_in[k]

    for d in range(1, nh):
        er_copy(d, h).wait_send()
        ea_copy(d, h).wait_send()
        for k in range(PIECES):
            y_copy(d, k).wait_send()
    for j in range(CUTS):
        core_copy(j).wait_send()
        for d in range(1, nx):
            xs_copy(d, j).wait_send()

    def i_end(d, carry):
        i_copy(d).wait_send()
        return carry

    lax.fori_loop(1, n, i_end, 0)

    def end_all(k, carry):
        @pl.when(k > z)
        def _():
            for j in range(CUTS):
                rin_copy(k, j).wait_send()

        @pl.when(k < z)
        def _():
            for j in range(CUTS):
                lin_copy(k, j).wait_send()

        for p in range(PIECES):

            @pl.when((k <= z) & (z + 1 < nz))
            def _(p=p):
                right_copy(k, p).wait_send()

            @pl.when((k >= z) & (z >= 1))
            def _(p=p):
                left_copy(k, p).wait_send()

            for dx in range(1, nx):
                x_copy(k, dx, p).wait_send()
            for xi in range(nx):
                c_copy(k, xi, p).wait_send()
        return carry

    lax.fori_loop(0, nz, end_all, 0)


def on_device(
    nz, nx,
    pooled, w_up, grad_out, owners, rows, lookup_weight, lens, slot_map,
    cache_weight, cache_accum, evict_slots, evict_dest, evict_count,
):
    tables, batch, bag = owners.shape
    slots = slot_map.shape[-1]
    rows_dev = slots // tables
    emb = cache_weight.shape[-1]
    n = lax.axis_size("tbl")
    nh = lax.axis_size("hst")
    feat_n, hid = w_up.shape
    out_rows = feat_n // n
    width = tables * emb
    groups = slots // emb
    list_len = evict_slots.shape[-1]
    cap = list_len // 2
    cut = hid // CUTS
    tile = min(512, hid)

    dma = pltpu.SemaphoreType.DMA
    vmem = pl.BlockSpec(memory_space=pltpu.VMEM)
    anyspace = pl.BlockSpec(memory_space=pl.ANY)
    i32 = jnp.int32
    grad_up, new_weight, new_accum, held_rows, held_accum = pl.pallas_call(
        functools.partial(step_kernel, nz, nx, nh, tables, rows_dev, tile),
        out_shape=(
            jax.ShapeDtypeStruct((out_rows, hid), F32),
            jax.ShapeDtypeStruct((slots, emb), F32),
            jax.ShapeDtypeStruct((groups, emb), F32),
            jax.ShapeDtypeStruct((nh, cap, emb), F32),
            jax.ShapeDtypeStruct((nh, 1, cap), F32),
        ),
        in_specs=[anyspace] * 13,
        out_specs=(vmem,) * 5,
        scratch_shapes=[
            pltpu.VMEM((batch, feat_n), BF16),
            pltpu.VMEM((feat_n, batch), BF16),
            pltpu.VMEM((feat_n, hid), BF16),
            pltpu.VMEM((batch, hid), BF16),
            pltpu.VMEM((batch, hid), BF16),
            pltpu.VMEM((tables, bag, batch), i32),
            pltpu.VMEM((tables, bag, batch), i32),
            pltpu.VMEM((tables, bag, batch), BF16),
            pltpu.VMEM((tables, batch), i32),
            pltpu.VMEM((1, slots), i32),
            pltpu.VMEM((slots, emb), F32),
            pltpu.VMEM((groups, emb), F32),
            pltpu.VMEM((1, list_len), i32),
            pltpu.VMEM((1, list_len), i32),
            pltpu.VMEM((1, 1), i32),
            pltpu.VMEM((batch, width), F32),
            pltpu.VMEM((nh - 1, batch, width), BF16),
            pltpu.VMEM((nh, batch, width), BF16),
            pltpu.VMEM((n, batch, width), BF16),
            pltpu.VMEM((n, tables, batch), F32),
            pltpu.VMEM((n, tables, batch), F32),
            pltpu.VMEM((CUTS, nz, nx, 2, out_rows, cut), F32),
            pltpu.VMEM((CUTS, nz, nx, out_rows, cut), F32),
            pltpu.VMEM((nz, CUTS, nx, out_rows, cut), BF16),
            pltpu.VMEM((nz, CUTS, nx, out_rows, cut), BF16),
            pltpu.VMEM((nz, CUTS, nx, out_rows, cut), BF16),
            pltpu.VMEM((max(nx - 1, 1), CUTS, out_rows, cut), BF16),
            pltpu.VMEM((nx, CUTS, out_rows, cut), BF16),
            pltpu.VMEM((slots, emb), F32),
            pltpu.VMEM((slots, emb), F32),
            pltpu.VMEM((groups, emb), i32),
            pltpu.VMEM((nh, cap), i32),
            pltpu.SMEM((groups, emb), i32),
            pltpu.SMEM((nh, cap), i32),
            pltpu.VMEM((nh, cap, emb), F32),
            pltpu.VMEM((nh, cap, emb), F32),
            pltpu.VMEM((nh, cap, emb), F32),
            pltpu.VMEM((nh, cap, emb), F32),
            pltpu.VMEM((nh, 1, cap), F32),
            pltpu.VMEM((nh, cap, emb), F32),
            pltpu.VMEM((nh, 1, cap), F32),
            dma((1 + hid // tile + BLOCKS + 10,)), dma((2,)),
            dma((nh, PIECES)), dma((nh, PIECES)), dma((n,)), dma((n,)),
            dma((nz, PIECES)), dma((nz, PIECES)), dma((nz, nx, PIECES)), dma((nz, nx, PIECES)),
            dma((n, PIECES)), dma((CUTS,)), dma((CUTS,)),
            dma((nz, CUTS)), dma((nz, CUTS)), dma((nz, CUTS)),
            dma((nx, CUTS)), dma((nx, CUTS)),
            dma((nh,)), dma((nh,)), dma((nh,)), dma((nh,)),
        ],
        compiler_params=pltpu.CompilerParams(
            collective_id=0, has_side_effects=True, vmem_limit_bytes=56 * 1024 * 1024
        ),
        name="step",
    )(
        pooled, w_up, grad_out,
        jnp.transpose(owners, (0, 2, 1)), jnp.transpose(rows, (0, 2, 1)),
        jnp.transpose(lookup_weight, (0, 2, 1)), lens, slot_map.reshape(1, slots),
        cache_weight.reshape(slots, emb), cache_accum.reshape(groups, emb),
        evict_slots.reshape(1, list_len), evict_dest.reshape(1, list_len), evict_count,
    )
    return (
        grad_up,
        new_weight[None, None],
        new_accum.reshape(1, 1, slots),
        held_rows[None, None],
        held_accum.reshape(1, 1, nh, cap),
    )


def solution(mesh):
    n, nh = mesh.shape["tbl"], mesh.shape["hst"]
    nx = nh if n % (2 * nh) == 0 else 1
    nz = n // (2 * nx)
    placed = (
        P("tbl", None),
        P(None, "hst"),
        P("tbl", "hst"),
        P("hst", "tbl", None),
        P("hst", "tbl", None),
        P("hst", "tbl", None),
        P("hst", "tbl"),
        P("tbl", "hst", None),
        P("tbl", "hst", None, None),
        P("tbl", "hst", None),
        P("tbl", "hst", None),
        P("tbl", "hst", None),
        P("tbl", "hst"),
    )
    return jax.shard_map(
        functools.partial(on_device, nz, nx),
        mesh=mesh,
        in_specs=placed,
        out_specs=(
            P("tbl", "hst"),
            P("tbl", "hst", None, None),
            P("tbl", "hst", None),
            P("tbl", "hst", None, None, None),
            P("tbl", "hst", None, None),
        ),
        check_vma=False,
    )
```

```python
import functools

import jax
import jax.numpy as jnp
from jax import lax
from jax.experimental import pallas as pl
from jax.experimental.pallas import tpu as pltpu
from jax.sharding import PartitionSpec as P

LEARN_RATE = 0.05
EPSILON = 1e-08
MESH = pl.DeviceIdType.MESH
BLOCKS = 2
SUBS = 2
PIECES = BLOCKS * SUBS
CUTS = 4
UPDATE_TILES = 4
RADIX = 256
ROW_STEP = 2048.0
WEIGHT_STEP = 512.0
F32 = jnp.float32
BF16 = jnp.bfloat16
NT_DIMS = (((1,), (1,)), ((), ()))


def iota(shape, axis):
    return lax.broadcasted_iota(jnp.int32, shape, axis)


def step_kernel(
    nz, nx, nh, tables, rows_dev, tile,
    pooled, w_up, grad_out, owners, rows, lookup_weight, lens, slot_map,
    weight, accum, evict_slots, evict_dest, evict_count,
    grad_up_o, new_weight_o, new_accum_o, held_rows_o, held_accum_o,
    grad_up, new_weight, new_accum, pooled_v, pooled_t, w_v, go_v, delta, own_v, row_v, lw_v, len_v, map_v, weight_v, accum_v,
    es_v, ed_v,
    fown, fsend, ybuf, gat, idx, idxb, grad, rcore, chain, rin, lin, xs, xr, place,
    wide, inv_v, src_v, inv_s, src_s, ev_s, ev_w, ev_a, ev_g, ev_rows, ev_acc, rows_in, acc_in,
    ld_s, sm_s, y_s, y_r, i_s, i_r, azr_s, azl_s, ax_s, ac_s, g_r, gc_r, rc_s, rc_r,
    ch_s, ci_r, xs_s, xr_r, er_s, er_r, ea_s, ea_r, out_s, w_s,
):
    n = nz * nx * 2
    me = lax.axis_index("tbl")
    h = lax.axis_index("hst")
    c = lax.rem(me, 2)
    zx = me // 2
    x = lax.rem(zx, nx)
    z = zx // nx
    other = 1 - c
    batch, hid = grad_out.shape
    feat_n = pooled.shape[1]
    width = ybuf.shape[-1]
    emb = width // tables
    bag = owners.shape[1]
    slots = weight.shape[0]
    list_len = evict_slots.shape[1]
    cap = ev_rows.shape[1]
    out_rows = grad.shape[4]
    cut = hid // CUTS
    piece = batch // PIECES
    block = batch // BLOCKS
    tiles = hid // tile

    def at(zi, xi, ci):
        return (zi * nx + xi) * 2 + ci

    def xof(d):
        return lax.rem(x + d, nx)

    def rcopy(src, dst, s, r, dev):
        return pltpu.make_async_remote_copy(
            src_ref=src, dst_ref=dst, send_sem=s, recv_sem=r,
            device_id=dev, device_id_type=MESH,
        )

    def cols(hh):
        return pl.ds(pl.multiple_of(hh * width, width), width)

    def span(k):
        return pl.ds(k * piece, piece)

    def spanb(k):
        return pl.ds(k * block, block)

    def cutcols(j):
        return pl.ds(j * cut, cut)

    loads = [pltpu.make_async_copy(pooled, pooled_v, ld_s.at[0])]
    w_loads = [
        pltpu.make_async_copy(
            w_up.at[:, pl.ds(j * tile, tile)], w_v.at[:, pl.ds(j * tile, tile)], ld_s.at[1 + j]
        )
        for j in range(tiles)
    ]
    g_loads = [
        pltpu.make_async_copy(grad_out.at[spanb(k)], go_v.at[spanb(k)], ld_s.at[1 + tiles + k])
        for k in range(BLOCKS)
    ]
    base = 1 + tiles + BLOCKS
    small = [
        pltpu.make_async_copy(src, dst, ld_s.at[base + k])
        for k, (src, dst) in enumerate((
            (owners, own_v), (rows, row_v), (lookup_weight, lw_v), (lens, len_v),
            (slot_map, map_v), (evict_slots, es_v), (evict_dest, ed_v),
            (accum, accum_v), (weight, weight_v),
        ))
    ]
    loads[0].start()
    w_loads[0].start()
    g_loads[0].start()
    barrier = pltpu.get_barrier_semaphore()

    def greet(d, carry):
        pl.semaphore_signal(
            barrier, inc=1, device_id={"tbl": lax.rem(me + d, n)}, device_id_type=MESH
        )
        return carry

    lax.fori_loop(1, n, greet, 0)
    for d in range(1, nh):
        pl.semaphore_signal(
            barrier, inc=1, device_id={"hst": lax.rem(h + d, nh)}, device_id_type=MESH
        )
    for copy in w_loads[1:] + g_loads[1:]:
        copy.start()

    def y_copy(d, k):
        h2 = lax.rem(h + d, nh)
        return rcopy(
            fsend.at[d - 1, span(k)], ybuf.at[h, span(k)], y_s, y_r.at[nh - d - 1, k], {"hst": h2}
        )

    def y_arrival(d, k):
        h2 = lax.rem(h + d, nh)
        return rcopy(
            fsend.at[d - 1, span(k)], ybuf.at[h2, span(k)], y_s, y_r.at[d - 1, k],
            {"hst": h2},
        )

    def deltas(k):
        g_loads[k].wait()
        for j in range(tiles):
            if k == 0:
                w_loads[j].wait()
            cs = pl.ds(j * tile, tile)
            p = jnp.dot(pooled_v[spanb(k), :], w_v[:, cs], preferred_element_type=F32)
            s = jax.nn.sigmoid(p)
            g = go_v[spanb(k), cs].astype(F32)
            delta[spanb(k), cs] = (g * s * (1.0 + p * (1.0 - s))).astype(BF16)

    def feats_out(k):
        for d in range(1, nh):
            h2 = lax.rem(h + d, nh)
            part = lax.dot_general(
                delta[spanb(k), :], w_v[cols(h2), :], NT_DIMS, preferred_element_type=F32
            )
            fsend[d - 1, spanb(k)] = part.astype(BF16)
            if k == 0 and d == 1:
                pl.semaphore_wait(barrier, n - 1 + nh - 1)
            for q in range(SUBS):
                y_copy(d, k * SUBS + q).start()

    def feats_own(k):
        fown[spanb(k), :] = lax.dot_general(
            delta[spanb(k), :], w_v[cols(h), :], NT_DIMS, preferred_element_type=F32
        )

    loads[0].wait()
    deltas(0)
    feats_out(0)
    for copy in small:
        copy.start()
    feats_own(0)
    deltas(1)
    feats_out(1)
    feats_own(1)

    def g_copy(slot, k, sem, dev):
        ref = gat.at[slot, span(k)]
        return rcopy(ref, ref, sem, g_r.at[slot // 2, k], {"tbl": dev})


    def right_copy(zi, k):
        return g_copy(at(zi, x, c), k, azr_s, at(z + 1, x, c))

    def left_copy(zi, k):
        return g_copy(at(zi, x, c), k, azl_s, at(z - 1, x, c))

    def x_copy(zi, d, k):
        return g_copy(at(zi, x, c), k, ax_s, at(z, xof(d), c))

    def c_copy(zi, xi, k):
        ref = gat.at[at(zi, xi, c), span(k)]
        return rcopy(ref, ref, ac_s, gc_r.at[zi * nx + xi], {"tbl": at(z, x, other)})

    def arrived(slot, k):
        g_copy(slot, k, ac_s, at(z, x, other)).wait_recv()

    def gather_start(k):
        total = fown[span(k), :]
        for d in range(1, nh):
            y_arrival(d, k).wait_recv()
            total = total + ybuf[lax.rem(h + d, nh), span(k)].astype(F32)
        gat[me, span(k)] = total.astype(BF16)

        @pl.when(z + 1 < nz)
        def _():
            right_copy(z, k).start()

        @pl.when(z >= 1)
        def _():
            left_copy(z, k).start()

        for d in range(1, nx):
            x_copy(z, d, k).start()
        c_copy(z, x, k).start()

    def core_copy(j):
        return rcopy(
            grad.at[j, :, :, other], rcore.at[j], rc_s, rc_r, {"tbl": at(z, x, other)}
        )

    def weight_grad(j):
        part = jnp.dot(pooled_t[...], delta[:, cutcols(j)], preferred_element_type=F32)
        grad[j] = part.reshape(nz, nx, 2, out_rows, cut)
        core_copy(j).start()

    def i_copy(d):
        o = lax.rem(me + d, n)
        return rcopy(idx.at[o], idxb.at[me], i_s, i_r.at[zx], {"tbl": o})

    def i_arrival(first, count):
        ref = idxb.at[pl.ds(first, count)]
        return rcopy(ref, ref, i_s, i_r.at[first // 2], {"tbl": at(z, x, other)})

    gather_start(0)
    for copy in small:
        copy.wait()
    for t in range(tables):
        used = iota((bag, batch), 0) < len_v[t : t + 1, :]
        code = (row_v[t] + 1).astype(F32) * ROW_STEP + lw_v[t].astype(F32) * WEIGHT_STEP
        code = jnp.where(used, code, 0.0)
        for o in range(n):
            idx[o, t : t + 1, :] = jnp.sum(
                jnp.where(own_v[t] == o, code, 0.0), axis=0, keepdims=True
            )
    idxb[me] = idx[me]

    def i_start(d, carry):
        i_copy(d).start()
        return carry

    lax.fori_loop(1, n, i_start, 0)
    pooled_t[...] = pooled_v[...].T

    weight_grad(0)
    for k in range(1, PIECES):
        gather_start(k)
        weight_grad(k)

    place[...] = jnp.zeros_like(place)
    chunk = min(RADIX, rows_dev)

    def proc(*picked):
        codes = [idxb[slot] for slot in picked]
        bags = [gat[slot] for slot in picked]
        for t in range(tables):
            pairs = []
            for code, bag_rows in zip(codes, bags):
                code = code[t : t + 1, :]
                row1 = jnp.floor(code * (1.0 / ROW_STEP))
                wgt = ((code - row1 * ROW_STEP) * (1.0 / WEIGHT_STEP)).astype(BF16)
                pairs.append((row1 - 1.0, wgt, bag_rows[:, t * emb : (t + 1) * emb]))
            ids = iota((chunk, batch), 0).astype(F32).astype(BF16)
            for r0 in range(0, rows_dev, chunk):
                total = None
                for row, wgt, part in pairs:
                    near = row - float(r0)
                    near = jnp.where((near >= 0.0) & (near < float(chunk)), near, -1.0)
                    mark = jnp.where(ids == near.astype(BF16), wgt, jnp.zeros((), BF16))
                    prod = jnp.dot(mark, part, preferred_element_type=F32)
                    total = prod if total is None else total + prod
                place[pl.ds(t * rows_dev + r0, chunk), :] += total

    eye = iota((emb, emb), 0) == iota((emb, emb), 1)
    groups = slots // emb

    inv_copy = pltpu.make_async_copy(inv_v, inv_s, sm_s.at[0])
    src_copy = pltpu.make_async_copy(src_v, src_s, sm_s.at[1])

    def prepare_inverse():
        home = map_v[...].astype(F32)
        high = jnp.floor(home * (1.0 / emb))
        low = home - high * emb
        from_row = iota((1, slots), 1).astype(F32)
        from_high = jnp.floor(from_row * (1.0 / RADIX))
        from_low = from_row - from_high * RADIX
        in_group = iota((groups, slots), 0).astype(F32) == high
        left = jnp.concatenate(
            [jnp.where(in_group, from_high, 0.0), jnp.where(in_group, from_low, 0.0)], axis=0
        ).astype(BF16)
        right = jnp.where(iota((emb, slots), 0).astype(F32) == low, 1.0, 0.0).astype(BF16)
        found = lax.dot_general(left, right, NT_DIMS, preferred_element_type=F32)
        inv = (found[:groups] * RADIX + found[groups:]).astype(jnp.int32)
        inv_v[...] = jnp.clip(inv, 0, slots - 1)
        inv_copy.start()


    def prepare_wide():
        for i in range(groups):
            col = jnp.sum(jnp.where(eye, accum_v[i : i + 1, :], 0.0), axis=1, keepdims=True)
            wide[i * emb : (i + 1) * emb, :] = jnp.broadcast_to(col, (emb, emb))

    def prepare_evict():
        live = iota((1, list_len), 1) < evict_count[0, 0]
        lanes = 8 * -(-nh // 8)
        mine = jnp.where((iota((lanes, list_len), 0) == ed_v[...]) & live, 1.0, 0.0)
        before = jnp.where(iota((list_len, list_len), 0) < iota((list_len, list_len), 1), 1.0, 0.0)
        goal = jnp.dot(mine.astype(BF16), before.astype(BF16), preferred_element_type=F32)
        slot1 = es_v[...].astype(F32) + 1.0
        slot_high = jnp.floor(slot1 * (1.0 / RADIX))
        slot_low = slot1 - slot_high * RADIX
        parts = jnp.where(iota((8, list_len), 0) == 0, slot_high, slot_low).astype(BF16)
        for d in range(nh):
            hot = jnp.where(
                iota((cap, list_len), 0).astype(F32) == goal[d : d + 1], mine[d : d + 1], 0.0
            ).astype(BF16)
            got = lax.dot_general(parts, hot, NT_DIMS, preferred_element_type=F32)
            src = (got[0:1] * RADIX + got[1:2]).astype(jnp.int32)
            src_v[d : d + 1, :] = jnp.clip(src, 0, slots)
        src_copy.start()


    def prepare_fetch(start, stop):
        def slot_of(k, p):
            s1 = src_s[k, p]
            return s1 > 0, jnp.maximum(s1 - 1, 0)

        def ev_fetch(i, carry):
            k = i // (cap // 8)
            p = lax.rem(i, cap // 8) * 8
            for q in range(8):
                ok, s = slot_of(k, p + q)
                ev_w[k, pl.ds(p + q, 1), :] = jnp.where(ok, weight_v[pl.ds(s, 1), :], 0.0)
                ev_a[k, pl.ds(p + q, 1), :] = jnp.where(ok, wide[pl.ds(s, 1), :], 0.0)
                ev_s[k, p + q] = jnp.where(ok, inv_s[s // emb, lax.rem(s, emb)], slots)
            return carry

        lax.fori_loop(start, stop, ev_fetch, 0)

    def rin_copy(t, j):
        return rcopy(
            chain.at[t, j], rin.at[t, j], ch_s, ci_r.at[t, j], {"tbl": at(z + 1, x, c)}
        )

    def lin_copy(t, j):
        return rcopy(
            chain.at[t, j], lin.at[t, j], ch_s, ci_r.at[jnp.where(t == z - 1, nz, t), j],
            {"tbl": at(z - 1, x, c)},
        )

    def lin_arrival(t, j):
        return rcopy(
            chain.at[t, j], lin.at[t, j], ch_s, ci_r.at[jnp.where(t == z, nz, t), j],
            {"tbl": at(z - 1, x, c)},
        )

    def own_sum(t, j, xi):
        return grad[j, t, xi, c] + rcore[j, t, xi]

    def chain_step(t, j, buf, copy):
        for xi in range(nx):
            s = own_sum(t, j, xi)
            if buf is not None:
                s = s + buf[t, j, xi].astype(F32)
            chain[t, j, xi] = s.astype(BF16)
        copy(t, j).start()


    def chain_heads():
        rcopy(rcore, rcore, rc_s, rc_r, {"tbl": at(z, x, other)}).wait_recv()

        @pl.when(z == 0)
        def _():
            def body(i, carry):
                for j in range(CUTS):
                    chain_step(nz - 1 - i, j, None, rin_copy)
                return carry

            lax.fori_loop(0, nz - 1, body, 0)

        @pl.when(z == nz - 1)
        def _():
            def body(i, carry):
                for j in range(CUTS):
                    chain_step(i, j, None, lin_copy)
                return carry

            lax.fori_loop(0, nz - 1, body, 0)

    def xs_copy(d, j):
        x2 = xof(d)
        return rcopy(xs.at[d - 1, j], xr.at[x, j], xs_s, xr_r.at[nx - d - 1], {"tbl": at(z, x2, c)})

    def xs_arrival(d):
        x2 = xof(d)
        return rcopy(xs.at[d - 1], xr.at[x2], xs_s, xr_r.at[d - 1], {"tbl": at(z, x2, c)})

    def finish_cut(j):
        @pl.when(z >= 1)
        def _():
            rin_copy(z, j).wait_recv()
            for xi in range(nx):
                grad[j, z, xi, c] += rin[z, j, xi].astype(F32)

        @pl.when(z + 1 < nz)
        def _():
            lin_arrival(z, j).wait_recv()
            for xi in range(nx):
                grad[j, z, xi, c] += lin[z, j, xi].astype(F32)

        for d in range(1, nx):
            xs[d - 1, j] = own_sum(z, j, xof(d)).astype(BF16)
            xs_copy(d, j).start()

    def from_z(zi, k, open_end, onward):
        arrived(at(zi, x, c), k)

        @pl.when(open_end)
        def _():
            onward(zi, k).start()

        for dx in range(1, nx):
            x_copy(zi, dx, k).start()
        c_copy(zi, x, k).start()

    both = jnp.minimum(z, nz - 1 - z)

    def ring(e):
        dist = (e + 1) // 2
        near = jnp.where(lax.rem(e, 2) == 1, z - dist, z + dist)
        dist = e - both
        far = jnp.where(z - dist >= 0, z - dist, z + dist)
        return jnp.where(e <= 2 * both, near, far)

    def from_x(i):
        head = i < PIECES
        i2 = i - PIECES
        paired = i2 < 2 * PIECES * both
        r = lax.rem(i2, 2 * PIECES)
        i3 = i2 - 2 * PIECES * both
        e = jnp.where(
            head, 0,
            jnp.where(
                paired, 1 + 2 * (i2 // (2 * PIECES)) + lax.rem(r, 2), 1 + 2 * both + i3 // PIECES
            ),
        )
        k = jnp.where(head, i, jnp.where(paired, r // 2, lax.rem(i3, PIECES)))
        zi = ring(e)
        for dx in range(1, nx):
            arrived(at(zi, xof(dx), c), k)
            c_copy(zi, xof(dx), k).start()

    def expect(zi, xi):
        mine = at(zi, xi, c)

        @pl.when(mine != me)
        def _():
            i_arrival(at(zi, xi, 0), 2).wait_recv()

        @pl.when(mine == me)
        def _():
            i_arrival(at(zi, xi, 0), 1).wait_recv()

        return mine

    def core_slot(zi, xi):
        slot = at(zi, xi, other)
        ref = gat.at[slot]
        rcopy(ref, ref, ac_s, gc_r.at[zi * nx + xi], {"tbl": at(z, x, other)}).wait_recv()
        return slot

    def pair_proc(zi, xi):
        mine = expect(zi, xi)
        proc(mine, core_slot(zi, xi))

    zr = nz - 1 - z

    def step_body(i, carry):
        j = i // PIECES + 1
        k = lax.rem(i, PIECES)
        s = j - 1

        @pl.when(z - j >= 0)
        def _():
            from_z(z - j, k, z + 1 < nz, right_copy)

        @pl.when(z + j < nz)
        def _():
            from_z(z + j, k, z >= 1, left_copy)

        from_x(i)

        @pl.when((s <= nz - 2) & (z >= 1) & (z <= s))
        def _():
            t = nz - 1 - s + z
            rin_copy(t, k).wait_recv()
            chain_step(t, k, rin, rin_copy)

        @pl.when((s <= nz - 2) & (zr >= 1) & (zr <= s))
        def _():
            t = s - zr
            lin_arrival(t, k).wait_recv()
            chain_step(t, k, lin, lin_copy)

        @pl.when(s == nz - 1)
        def _():
            finish_cut(k)

        @pl.when(i == 1)
        def _():
            chain_heads()
            prepare_inverse()

        @pl.when(i == 2)
        def _():
            prepare_wide()

        @pl.when(i == 3)
        def _():
            prepare_evict()

        @pl.when(i == 2 * PIECES - 1)
        def _():
            inv_copy.wait()
            src_copy.wait()
            prepare_fetch(0, nh * cap // 16)

        @pl.when(i == 3 * PIECES - 1)
        def _():
            prepare_fetch(nh * cap // 16, nh * cap // 8)

        side = lax.rem(k, 2) == 0
        near = k < 2
        zi = jnp.where(near, jnp.where(side, z - s, z + s), ring(jnp.maximum(s - 1, 0)))
        on_line = near & ((s >= 1) | side) & (zi >= 0) & (zi < nz)
        on_side = (k == 2) & (s >= 1)

        @pl.when(on_line | on_side)
        def _():
            def one(dx, carry):
                pair_proc(zi, xof(dx))
                return carry

            lax.fori_loop(jnp.where(near, 0, 1), jnp.where(near, 1, nx), one, 0)

        return carry

    lax.fori_loop(0, PIECES * nz, step_body, 0)
    for dx in range(1, nx):
        proc(expect(ring(nz - 1), xof(dx)))
        proc(core_slot(ring(nz - 1), xof(dx)))

    def gathered(first):
        picks = []
        for q in range(8):
            picks.append(place[pl.ds(first(q), 1), :])
        return jnp.concatenate(picks, axis=0)

    def ev_gather(i, carry):
        k = i // (cap // 8)
        p = lax.rem(i, cap // 8) * 8
        ev_g[k, pl.ds(pl.multiple_of(p, 8), 8), :] = gathered(lambda q: ev_s[k, p + q])
        return carry

    lax.fori_loop(0, nh * cap // 8, ev_gather, 0)

    def er_copy(d, slot):
        k = lax.rem(h + d, nh)
        return rcopy(ev_rows.at[k], rows_in.at[slot], er_s, er_r.at[slot], {"hst": k})

    def ea_copy(d, slot):
        k = lax.rem(h + d, nh)
        return rcopy(ev_acc.at[k], acc_in.at[slot], ea_s, ea_r.at[slot], {"hst": k})

    for d in range(1, nh + 1):
        k = lax.rem(h + d, nh)
        for r0 in range(0, cap, emb):
            span_k = pl.ds(r0, emb)
            g = ev_g[k, span_k]
            acc = ev_a[k, span_k] + jnp.mean(g * g, axis=1, keepdims=True)
            ev_rows[k, span_k] = ev_w[k, span_k] - LEARN_RATE * g / (jnp.sqrt(acc) + EPSILON)
            ev_acc[k, :, span_k] = jnp.sum(jnp.where(eye, acc, 0.0), axis=0, keepdims=True)
        if d < nh:
            er_copy(d, h).start()
            ea_copy(d, h).start()
    def held_out(buf, acc, k):
        return (
            pltpu.make_async_copy(buf.at[k], held_rows_o.at[k], out_s.at[2 + k]),
            pltpu.make_async_copy(acc.at[k], held_accum_o.at[k], out_s.at[2 + nh + k]),
        )

    for copy in held_out(ev_rows, ev_acc, h):
        copy.start()

    batch_tiles = max(u for u in (1, 2, UPDATE_TILES) if groups % u == 0)
    spread = batch_tiles * emb

    def weight_out(i):
        at_i = pl.ds(pl.multiple_of(i * spread, spread), spread)
        return pltpu.make_async_copy(new_weight.at[at_i], new_weight_o.at[at_i], w_s)

    def update(i2, carry):
        for u in range(batch_tiles):
            i = i2 * batch_tiles + u
            total = jnp.zeros((8, emb), F32)
            for b in range(emb // 8):
                rows_b = pl.ds(pl.multiple_of(i * emb + b * 8, 8), 8)
                g = gathered(lambda q: inv_s[i, b * 8 + q])
                acc = wide[rows_b, :] + jnp.mean(g * g, axis=1, keepdims=True)
                new_weight[rows_b, :] = weight_v[rows_b, :] - LEARN_RATE * g / (
                    jnp.sqrt(acc) + EPSILON
                )
                diag = iota((8, emb), 1) == iota((8, emb), 0) + b * 8
                total = total + jnp.where(diag, acc, 0.0)
            new_accum[pl.ds(i, 1), :] = jnp.sum(total, axis=0, keepdims=True)
        weight_out(i2).start()
        return carry

    lax.fori_loop(0, groups // batch_tiles, update, 0)
    accum_out = pltpu.make_async_copy(new_accum, new_accum_o, out_s.at[0])
    accum_out.start()

    for d in range(1, nx):
        xs_arrival(d).wait_recv()
    for j in range(CUTS):
        s = own_sum(z, j, x)
        for d in range(1, nx):
            s = s + xr[xof(d), j].astype(F32)
        grad_up[:, cutcols(j)] = s
    grad_out_copy = pltpu.make_async_copy(grad_up, grad_up_o, out_s.at[1])
    grad_out_copy.start()

    for d in range(1, nh):
        k = lax.rem(h + d, nh)
        er_copy(d, k).wait_recv()
        ea_copy(d, k).wait_recv()
        for copy in held_out(rows_in, acc_in, k):
            copy.start()

    def all_sent(ref, sem, recv, dev):
        rcopy(ref, ref, sem, recv, dev).wait_send()

    core_dev = {"tbl": at(z, x, other)}
    if nh > 1:
        host_dev = {"hst": lax.rem(h + 1, nh)}
        all_sent(ev_rows.at[pl.ds(0, nh - 1)], er_s, er_r.at[0], host_dev)
        all_sent(ev_acc.at[pl.ds(0, nh - 1)], ea_s, ea_r.at[0], host_dev)
        all_sent(fsend, y_s, y_r.at[0, 0], host_dev)
    all_sent(rcore, rc_s, rc_r, core_dev)
    all_sent(idx.at[pl.ds(0, n - 1)], i_s, i_r.at[0], core_dev)
    all_sent(gat.at[pl.ds(0, nz * nx)], ac_s, gc_r.at[0], core_dev)
    if nx > 1:
        all_sent(xs, xs_s, xr_r.at[0], core_dev)
        all_sent(gat.at[pl.ds(0, nz * (nx - 1))], ax_s, gc_r.at[0], core_dev)
    if nz > 1:
        all_sent(chain.at[pl.ds(0, nz - 1)], ch_s, ci_r.at[0, 0], core_dev)
    for q in range(nz - 1):

        @pl.when(z == q)
        def _(q=q):
            all_sent(gat.at[pl.ds(0, q + 1)], azr_s, gc_r.at[0], core_dev)

        @pl.when(zr == q)
        def _(q=q):
            all_sent(gat.at[pl.ds(0, q + 1)], azl_s, gc_r.at[0], core_dev)

    pltpu.make_async_copy(new_weight, new_weight_o, w_s).wait()
    accum_out.wait()
    grad_out_copy.wait()
    for d in range(nh):
        k = lax.rem(h + d, nh)
        buf, acc = (ev_rows, ev_acc) if d == 0 else (rows_in, acc_in)
        for copy in held_out(buf, acc, k):
            copy.wait()


def write_kernel(*refs):
    sems = refs[10]
    copies = [pltpu.make_async_copy(refs[k], refs[5 + k], sems.at[k]) for k in range(5)]
    for copy in copies:
        copy.start()
    for copy in copies:
        copy.wait()


def on_device(
    nz, nx,
    pooled, w_up, grad_out, owners, rows, lookup_weight, lens, slot_map,
    cache_weight, cache_accum, evict_slots, evict_dest, evict_count,
):
    tables, batch, bag = owners.shape
    slots = slot_map.shape[-1]
    rows_dev = slots // tables
    emb = cache_weight.shape[-1]
    n = lax.axis_size("tbl")
    nh = lax.axis_size("hst")
    feat_n, hid = w_up.shape
    out_rows = feat_n // n
    width = tables * emb
    groups = slots // emb
    list_len = evict_slots.shape[-1]
    cap = list_len // 2
    cut = hid // CUTS
    tile = min(512, hid)

    dma = pltpu.SemaphoreType.DMA
    anyspace = pl.BlockSpec(memory_space=pltpu.HBM)
    i32 = jnp.int32
    grad_up, new_weight, new_accum, held_rows, held_accum = pl.pallas_call(
        functools.partial(step_kernel, nz, nx, nh, tables, rows_dev, tile),
        out_shape=(
            jax.ShapeDtypeStruct((out_rows, hid), F32),
            jax.ShapeDtypeStruct((slots, emb), F32),
            jax.ShapeDtypeStruct((groups, emb), F32),
            jax.ShapeDtypeStruct((nh, cap, emb), F32),
            jax.ShapeDtypeStruct((nh, 1, cap), F32),
        ),
        in_specs=[anyspace] * 12 + [pl.BlockSpec(memory_space=pltpu.SMEM)],
        out_specs=(pl.BlockSpec(memory_space=pl.ANY),) * 5,
        scratch_shapes=[
            pltpu.VMEM((out_rows, hid), F32),
            pltpu.VMEM((slots, emb), F32),
            pltpu.VMEM((groups, emb), F32),
            pltpu.VMEM((batch, feat_n), BF16),
            pltpu.VMEM((feat_n, batch), BF16),
            pltpu.VMEM((feat_n, hid), BF16),
            pltpu.VMEM((batch, hid), BF16),
            pltpu.VMEM((batch, hid), BF16),
            pltpu.VMEM((tables, bag, batch), i32),
            pltpu.VMEM((tables, bag, batch), i32),
            pltpu.VMEM((tables, bag, batch), BF16),
            pltpu.VMEM((tables, batch), i32),
            pltpu.VMEM((1, slots), i32),
            pltpu.VMEM((slots, emb), F32),
            pltpu.VMEM((groups, emb), F32),
            pltpu.VMEM((1, list_len), i32),
            pltpu.VMEM((1, list_len), i32),
            pltpu.VMEM((batch, width), F32),
            pltpu.VMEM((nh - 1, batch, width), BF16),
            pltpu.VMEM((nh, batch, width), BF16),
            pltpu.VMEM((n, batch, width), BF16),
            pltpu.VMEM((n, tables, batch), F32),
            pltpu.VMEM((n, tables, batch), F32),
            pltpu.VMEM((CUTS, nz, nx, 2, out_rows, cut), F32),
            pltpu.VMEM((CUTS, nz, nx, out_rows, cut), F32),
            pltpu.VMEM((nz, CUTS, nx, out_rows, cut), BF16),
            pltpu.VMEM((nz, CUTS, nx, out_rows, cut), BF16),
            pltpu.VMEM((nz, CUTS, nx, out_rows, cut), BF16),
            pltpu.VMEM((max(nx - 1, 1), CUTS, out_rows, cut), BF16),
            pltpu.VMEM((nx, CUTS, out_rows, cut), BF16),
            pltpu.VMEM((slots + 8, emb), F32),
            pltpu.VMEM((slots, emb), F32),
            pltpu.VMEM((groups, emb), i32),
            pltpu.VMEM((nh, cap), i32),
            pltpu.SMEM((groups, emb), i32),
            pltpu.SMEM((nh, cap), i32),
            pltpu.SMEM((nh, cap), i32),
            pltpu.VMEM((nh, cap, emb), F32),
            pltpu.VMEM((nh, cap, emb), F32),
            pltpu.VMEM((nh, cap, emb), F32),
            pltpu.VMEM((nh, cap, emb), F32),
            pltpu.VMEM((nh, 1, cap), F32),
            pltpu.VMEM((nh, cap, emb), F32),
            pltpu.VMEM((nh, 1, cap), F32),
            dma((1 + hid // tile + BLOCKS + 9,)), dma((2,)),
            dma, dma((max(nh - 1, 1), PIECES)), dma, dma((nz * nx,)),
            dma, dma, dma, dma, dma((nz * nx, PIECES)), dma((nz * nx,)), dma, dma,
            dma, dma((nz + 1, CUTS)), dma, dma((max(nx - 1, 1),)),
            dma, dma((nh,)), dma, dma((nh,)), dma((2 + 2 * nh,)), dma,
        ],
        compiler_params=pltpu.CompilerParams(
            collective_id=0, has_side_effects=True, vmem_limit_bytes=48 * 1024 * 1024
        ),
        name="step",
    )(*[pltpu.with_memory_space_constraint(v, pltpu.HBM) for v in (
        pooled, w_up, grad_out,
        jnp.transpose(owners, (0, 2, 1)), jnp.transpose(rows, (0, 2, 1)),
        jnp.transpose(lookup_weight, (0, 2, 1)), lens, slot_map.reshape(1, slots),
        cache_weight.reshape(slots, emb), cache_accum.reshape(groups, emb),
        evict_slots.reshape(1, list_len), evict_dest.reshape(1, list_len),
    )], evict_count)
    outs = (grad_up, new_weight, new_accum, held_rows, held_accum)
    hbm = pl.BlockSpec(memory_space=pltpu.HBM)
    grad_up, new_weight, new_accum, held_rows, held_accum = pl.pallas_call(
        write_kernel,
        out_shape=tuple(jax.ShapeDtypeStruct(v.shape, v.dtype) for v in outs),
        in_specs=[pl.BlockSpec(memory_space=pl.ANY)] * 5,
        out_specs=(hbm,) * 5,
        scratch_shapes=[dma((5,))],
        compiler_params=pltpu.CompilerParams(vmem_limit_bytes=1024 * 1024),
        name="write",
    )(*outs)
    return (
        grad_up,
        new_weight[None, None],
        new_accum.reshape(1, 1, slots),
        held_rows[None, None],
        held_accum.reshape(1, 1, nh, cap),
    )


def solution(mesh):
    n, nh = mesh.shape["tbl"], mesh.shape["hst"]
    nx = nh if n % (2 * nh) == 0 else 1
    nz = n // (2 * nx)
    placed = (
        P("tbl", None),
        P(None, "hst"),
        P("tbl", "hst"),
        P("hst", "tbl", None),
        P("hst", "tbl", None),
        P("hst", "tbl", None),
        P("hst", "tbl"),
        P("tbl", "hst", None),
        P("tbl", "hst", None, None),
        P("tbl", "hst", None),
        P("tbl", "hst", None),
        P("tbl", "hst", None),
        P("tbl", "hst"),
    )
    return jax.shard_map(
        functools.partial(on_device, nz, nx),
        mesh=mesh,
        in_specs=placed,
        out_specs=(
            P("tbl", "hst"),
            P("tbl", "hst", None, None),
            P("tbl", "hst", None),
            P("tbl", "hst", None, None, None),
            P("tbl", "hst", None, None),
        ),
        check_vma=False,
    )
```

```python
import functools

import jax
import jax.numpy as jnp
from jax import lax
from jax.experimental import pallas as pl
from jax.experimental.pallas import tpu as pltpu
from jax.sharding import PartitionSpec as P

LEARN_RATE = 0.05
EPSILON = 1e-08
MESH = pl.DeviceIdType.MESH
BLOCKS = 2
SUBS = 2
PIECES = BLOCKS * SUBS
CUTS = 4
UPDATE_TILES = 4
RADIX = 256
ROW_STEP = 2048.0
WEIGHT_STEP = 512.0
F32 = jnp.float32
BF16 = jnp.bfloat16
NT_DIMS = (((1,), (1,)), ((), ()))


def iota(shape, axis):
    return lax.broadcasted_iota(jnp.int32, shape, axis)


def step_kernel(
    nz, nx, nh, tables, rows_dev, tile,
    pooled, w_up, grad_out, owners, rows, lookup_weight, lens, slot_map,
    weight, accum, evict_slots, evict_dest, evict_count,
    grad_up_o, new_weight_o, new_accum_o, held_rows_o, held_accum_o,
    grad_up, new_weight, new_accum, pooled_v, pooled_t, w_v, go_v, delta, own_v, row_v, lw_v, len_v, map_v, weight_v, accum_v,
    es_v, ed_v,
    fown, fsend, ybuf, gat, idx, idxb, grad, rcore, chain, rin, lin, xs, xr, place,
    wide, inv_v, src_v, inv_s, src_s, ev_s, ev_w, ev_a, ev_g, ev_rows, ev_acc, rows_in, acc_in, ev_half, half_in,
    ld_s, sm_s, y_s, y_r, i_s, i_r, azr_s, azl_s, ax_s, ac_s, g_r, gc_r, rc_s, rc_r,
    ch_s, ci_r, xs_s, xr_r, er_s, er_r, ea_s, ea_r, out_s, w_s,
):
    n = nz * nx * 2
    me = lax.axis_index("tbl")
    h = lax.axis_index("hst")
    c = lax.rem(me, 2)
    zx = me // 2
    x = lax.rem(zx, nx)
    z = zx // nx
    other = 1 - c
    batch, hid = grad_out.shape
    feat_n = pooled.shape[1]
    width = ybuf.shape[-1]
    emb = width // tables
    bag = owners.shape[1]
    slots = weight.shape[0]
    list_len = evict_slots.shape[1]
    cap = ev_rows.shape[1]
    out_rows = grad.shape[4]
    cut = hid // CUTS
    piece = batch // PIECES
    block = batch // BLOCKS
    tiles = hid // tile

    def at(zi, xi, ci):
        return (zi * nx + xi) * 2 + ci

    def xof(d):
        return lax.rem(x + d, nx)

    def rcopy(src, dst, s, r, dev):
        return pltpu.make_async_remote_copy(
            src_ref=src, dst_ref=dst, send_sem=s, recv_sem=r,
            device_id=dev, device_id_type=MESH,
        )

    def cols(hh):
        return pl.ds(pl.multiple_of(hh * width, width), width)

    def span(k):
        return pl.ds(k * piece, piece)

    def spanb(k):
        return pl.ds(k * block, block)

    def cutcols(j):
        return pl.ds(j * cut, cut)

    loads = [pltpu.make_async_copy(pooled, pooled_v, ld_s.at[0])]
    w_loads = [
        pltpu.make_async_copy(
            w_up.at[:, pl.ds(j * tile, tile)], w_v.at[:, pl.ds(j * tile, tile)], ld_s.at[1 + j]
        )
        for j in range(tiles)
    ]
    g_loads = [
        pltpu.make_async_copy(grad_out.at[spanb(k)], go_v.at[spanb(k)], ld_s.at[1 + tiles + k])
        for k in range(BLOCKS)
    ]
    base = 1 + tiles + BLOCKS
    small = [
        pltpu.make_async_copy(src, dst, ld_s.at[base + k])
        for k, (src, dst) in enumerate((
            (owners, own_v), (rows, row_v), (lookup_weight, lw_v), (lens, len_v),
            (slot_map, map_v), (evict_slots, es_v), (evict_dest, ed_v),
            (accum, accum_v), (weight, weight_v),
        ))
    ]
    loads[0].start()
    w_loads[0].start()
    g_loads[0].start()
    barrier = pltpu.get_barrier_semaphore()

    def greet(d, carry):
        pl.semaphore_signal(
            barrier, inc=1, device_id={"tbl": lax.rem(me + d, n)}, device_id_type=MESH
        )
        return carry

    lax.fori_loop(1, n, greet, 0)
    for d in range(1, nh):
        pl.semaphore_signal(
            barrier, inc=1, device_id={"hst": lax.rem(h + d, nh)}, device_id_type=MESH
        )
    for copy in w_loads[1:] + small + g_loads[1:]:
        copy.start()

    def y_copy(d, k):
        h2 = lax.rem(h + d, nh)
        return rcopy(
            fsend.at[d - 1, span(k)], ybuf.at[h, span(k)], y_s, y_r.at[nh - d - 1, k], {"hst": h2}
        )

    def y_arrival(d, k):
        h2 = lax.rem(h + d, nh)
        return rcopy(
            fsend.at[d - 1, span(k)], ybuf.at[h2, span(k)], y_s, y_r.at[d - 1, k],
            {"hst": h2},
        )

    def deltas(k):
        g_loads[k].wait()
        for j in range(tiles):
            if k == 0:
                w_loads[j].wait()
            cs = pl.ds(j * tile, tile)
            p = jnp.dot(pooled_v[spanb(k), :], w_v[:, cs], preferred_element_type=F32)
            s = jax.nn.sigmoid(p)
            g = go_v[spanb(k), cs].astype(F32)
            delta[spanb(k), cs] = (g * s * (1.0 + p * (1.0 - s))).astype(BF16)

    def feats_out(k):
        for d in range(1, nh):
            h2 = lax.rem(h + d, nh)
            part = lax.dot_general(
                delta[spanb(k), :], w_v[cols(h2), :], NT_DIMS, preferred_element_type=F32
            )
            fsend[d - 1, spanb(k)] = part.astype(BF16)
            if k == 0 and d == 1:
                pl.semaphore_wait(barrier, n - 1 + nh - 1)
            y_copy(d, k * SUBS).start()

    def feats_rest(k):
        for q in range(1, SUBS):
            for d in range(1, nh):
                y_copy(d, k * SUBS + q).start()

    def feats_own(k):
        fown[spanb(k), :] = lax.dot_general(
            delta[spanb(k), :], w_v[cols(h), :], NT_DIMS, preferred_element_type=F32
        )

    def i_copy(d):
        o = lax.rem(me + d, n)
        return rcopy(idx.at[o], idxb.at[me], i_s, i_r.at[zx], {"tbl": o})

    def i_arrival(first, count):
        ref = idxb.at[pl.ds(first, count)]
        return rcopy(ref, ref, i_s, i_r.at[first // 2], {"tbl": at(z, x, other)})

    loads[0].wait()
    deltas(0)
    feats_out(0)
    for copy in small:
        copy.wait()
    for t in range(tables):
        used = iota((bag, batch), 0) < len_v[t : t + 1, :]
        code = (row_v[t] + 1).astype(F32) * ROW_STEP + lw_v[t].astype(F32) * WEIGHT_STEP
        code = jnp.where(used, code, 0.0)
        for o in range(n):
            idx[o, t : t + 1, :] = jnp.sum(
                jnp.where(own_v[t] == o, code, 0.0), axis=0, keepdims=True
            )
    idxb[me] = idx[me]

    def i_start(d, carry):
        i_copy(d).start()
        return carry

    lax.fori_loop(1, n, i_start, 0)

    feats_rest(0)
    feats_own(0)
    deltas(1)
    feats_out(1)
    feats_own(1)
    feats_rest(1)

    def g_copy(slot, k, sem, dev):
        ref = gat.at[slot, span(k)]
        return rcopy(ref, ref, sem, g_r.at[slot // 2, k], {"tbl": dev})


    def right_copy(zi, k):
        return g_copy(at(zi, x, c), k, azr_s, at(z + 1, x, c))

    def left_copy(zi, k):
        return g_copy(at(zi, x, c), k, azl_s, at(z - 1, x, c))

    def x_copy(zi, d, k):
        return g_copy(at(zi, x, c), k, ax_s, at(z, xof(d), c))

    def c_copy(zi, xi, k):
        ref = gat.at[at(zi, xi, c), span(k)]
        return rcopy(ref, ref, ac_s, gc_r.at[zi * nx + xi], {"tbl": at(z, x, other)})

    def arrived(slot, k):
        g_copy(slot, k, ac_s, at(z, x, other)).wait_recv()

    def gather_start(k):
        total = fown[span(k), :]
        for d in range(1, nh):
            y_arrival(d, k).wait_recv()
            total = total + ybuf[lax.rem(h + d, nh), span(k)].astype(F32)
        gat[me, span(k)] = total.astype(BF16)

        @pl.when(z + 1 < nz)
        def _():
            right_copy(z, k).start()

        @pl.when(z >= 1)
        def _():
            left_copy(z, k).start()

        for d in range(1, nx):
            x_copy(z, d, k).start()
        c_copy(z, x, k).start()

    def core_copy(j):
        return rcopy(
            grad.at[j, :, :, other], rcore.at[j], rc_s, rc_r, {"tbl": at(z, x, other)}
        )

    def weight_grad(j):
        part = jnp.dot(pooled_t[...], delta[:, cutcols(j)], preferred_element_type=F32)
        grad[j] = part.reshape(nz, nx, 2, out_rows, cut)
        core_copy(j).start()

    gather_start(0)
    pooled_t[...] = pooled_v[...].T
    weight_grad(0)
    for k in range(1, PIECES):
        gather_start(k)
        weight_grad(k)

    place[...] = jnp.zeros_like(place)
    chunk = min(RADIX, rows_dev)

    def proc(*picked):
        codes = [idxb[slot] for slot in picked]
        bags = [gat[slot] for slot in picked]
        for t in range(tables):
            pairs = []
            for code, bag_rows in zip(codes, bags):
                code = code[t : t + 1, :]
                row1 = jnp.floor(code * (1.0 / ROW_STEP))
                wgt = ((code - row1 * ROW_STEP) * (1.0 / WEIGHT_STEP)).astype(BF16)
                pairs.append((row1 - 1.0, wgt, bag_rows[:, t * emb : (t + 1) * emb]))
            ids = iota((chunk, batch), 0).astype(F32).astype(BF16)
            for r0 in range(0, rows_dev, chunk):
                total = None
                for row, wgt, part in pairs:
                    near = row - float(r0)
                    near = jnp.where((near >= 0.0) & (near < float(chunk)), near, -1.0)
                    mark = jnp.where(ids == near.astype(BF16), wgt, jnp.zeros((), BF16))
                    prod = jnp.dot(mark, part, preferred_element_type=F32)
                    total = prod if total is None else total + prod
                place[pl.ds(t * rows_dev + r0, chunk), :] += total

    eye = iota((emb, emb), 0) == iota((emb, emb), 1)
    groups = slots // emb

    inv_copy = pltpu.make_async_copy(inv_v, inv_s, sm_s.at[0])
    src_copy = pltpu.make_async_copy(src_v, src_s, sm_s.at[1])

    def prepare_inverse():
        home = map_v[...].astype(F32)
        high = jnp.floor(home * (1.0 / emb))
        low = home - high * emb
        from_row = iota((1, slots), 1).astype(F32)
        from_high = jnp.floor(from_row * (1.0 / RADIX))
        from_low = from_row - from_high * RADIX
        in_group = iota((groups, slots), 0).astype(F32) == high
        left = jnp.concatenate(
            [jnp.where(in_group, from_high, 0.0), jnp.where(in_group, from_low, 0.0)], axis=0
        ).astype(BF16)
        right = jnp.where(iota((emb, slots), 0).astype(F32) == low, 1.0, 0.0).astype(BF16)
        found = lax.dot_general(left, right, NT_DIMS, preferred_element_type=F32)
        inv = (found[:groups] * RADIX + found[groups:]).astype(jnp.int32)
        inv_v[...] = jnp.clip(inv, 0, slots - 1)
        inv_copy.start()


    def prepare_wide():
        for i in range(groups):
            col = jnp.sum(jnp.where(eye, accum_v[i : i + 1, :], 0.0), axis=1, keepdims=True)
            wide[i * emb : (i + 1) * emb, :] = jnp.broadcast_to(col, (emb, emb))

    def prepare_evict():
        live = iota((1, list_len), 1) < evict_count[0, 0]
        lanes = 8 * -(-nh // 8)
        mine = jnp.where((iota((lanes, list_len), 0) == ed_v[...]) & live, 1.0, 0.0)
        before = jnp.where(iota((list_len, list_len), 0) < iota((list_len, list_len), 1), 1.0, 0.0)
        goal = jnp.dot(mine.astype(BF16), before.astype(BF16), preferred_element_type=F32)
        slot1 = es_v[...].astype(F32) + 1.0
        slot_high = jnp.floor(slot1 * (1.0 / RADIX))
        slot_low = slot1 - slot_high * RADIX
        parts = jnp.where(iota((8, list_len), 0) == 0, slot_high, slot_low).astype(BF16)
        for d in range(nh):
            hot = jnp.where(
                iota((cap, list_len), 0).astype(F32) == goal[d : d + 1], mine[d : d + 1], 0.0
            ).astype(BF16)
            got = lax.dot_general(parts, hot, NT_DIMS, preferred_element_type=F32)
            src = (got[0:1] * RADIX + got[1:2]).astype(jnp.int32)
            src_v[d : d + 1, :] = jnp.clip(src, 0, slots)
        src_copy.start()


    def prepare_fetch(start, stop):
        def slot_of(k, p):
            s1 = src_s[k, p]
            return s1 > 0, jnp.maximum(s1 - 1, 0)

        def ev_fetch(i, carry):
            k = i // (cap // 8)
            p = lax.rem(i, cap // 8) * 8
            for q in range(8):
                ok, s = slot_of(k, p + q)
                ev_w[k, pl.ds(p + q, 1), :] = jnp.where(ok, weight_v[pl.ds(s, 1), :], 0.0)
                ev_a[k, pl.ds(p + q, 1), :] = jnp.where(ok, wide[pl.ds(s, 1), :], 0.0)
                ev_s[k, p + q] = jnp.where(ok, inv_s[s // emb, lax.rem(s, emb)], slots)
            return carry

        lax.fori_loop(start, stop, ev_fetch, 0)

    def rin_copy(t, j):
        return rcopy(
            chain.at[t, j], rin.at[t, j], ch_s, ci_r.at[t, j], {"tbl": at(z + 1, x, c)}
        )

    def lin_copy(t, j):
        return rcopy(
            chain.at[t, j], lin.at[t, j], ch_s, ci_r.at[jnp.where(t == z - 1, nz, t), j],
            {"tbl": at(z - 1, x, c)},
        )

    def lin_arrival(t, j):
        return rcopy(
            chain.at[t, j], lin.at[t, j], ch_s, ci_r.at[jnp.where(t == z, nz, t), j],
            {"tbl": at(z - 1, x, c)},
        )

    def own_sum(t, j, xi):
        return grad[j, t, xi, c] + rcore[j, t, xi]

    def chain_step(t, j, buf, copy):
        for xi in range(nx):
            s = own_sum(t, j, xi)
            if buf is not None:
                s = s + buf[t, j, xi].astype(F32)
            chain[t, j, xi] = s.astype(BF16)
        copy(t, j).start()


    def chain_heads():
        rcopy(rcore, rcore, rc_s, rc_r, {"tbl": at(z, x, other)}).wait_recv()

        @pl.when(z == 0)
        def _():
            def body(i, carry):
                for j in range(CUTS):
                    chain_step(nz - 1 - i, j, None, rin_copy)
                return carry

            lax.fori_loop(0, nz - 1, body, 0)

        @pl.when(z == nz - 1)
        def _():
            def body(i, carry):
                for j in range(CUTS):
                    chain_step(i, j, None, lin_copy)
                return carry

            lax.fori_loop(0, nz - 1, body, 0)

    def xs_copy(d, j):
        x2 = xof(d)
        return rcopy(xs.at[d - 1, j], xr.at[x, j], xs_s, xr_r.at[nx - d - 1], {"tbl": at(z, x2, c)})

    def xs_arrival(d):
        x2 = xof(d)
        return rcopy(xs.at[d - 1], xr.at[x2], xs_s, xr_r.at[d - 1], {"tbl": at(z, x2, c)})

    def finish_cut(j):
        @pl.when(z >= 1)
        def _():
            rin_copy(z, j).wait_recv()
            for xi in range(nx):
                grad[j, z, xi, c] += rin[z, j, xi].astype(F32)

        @pl.when(z + 1 < nz)
        def _():
            lin_arrival(z, j).wait_recv()
            for xi in range(nx):
                grad[j, z, xi, c] += lin[z, j, xi].astype(F32)

        for d in range(1, nx):
            xs[d - 1, j] = own_sum(z, j, xof(d)).astype(BF16)
            xs_copy(d, j).start()

    def from_z(zi, k, open_end, onward):
        arrived(at(zi, x, c), k)

        @pl.when(open_end)
        def _():
            onward(zi, k).start()

        for dx in range(1, nx):
            x_copy(zi, dx, k).start()
        c_copy(zi, x, k).start()

    both = jnp.minimum(z, nz - 1 - z)

    def ring(e):
        dist = (e + 1) // 2
        near = jnp.where(lax.rem(e, 2) == 1, z - dist, z + dist)
        dist = e - both
        far = jnp.where(z - dist >= 0, z - dist, z + dist)
        return jnp.where(e <= 2 * both, near, far)

    def from_x(i):
        head = i < PIECES
        i2 = i - PIECES
        paired = i2 < 2 * PIECES * both
        r = lax.rem(i2, 2 * PIECES)
        i3 = i2 - 2 * PIECES * both
        e = jnp.where(
            head, 0,
            jnp.where(
                paired, 1 + 2 * (i2 // (2 * PIECES)) + lax.rem(r, 2), 1 + 2 * both + i3 // PIECES
            ),
        )
        k = jnp.where(head, i, jnp.where(paired, r // 2, lax.rem(i3, PIECES)))
        zi = ring(e)
        for dx in range(1, nx):
            arrived(at(zi, xof(dx), c), k)
            c_copy(zi, xof(dx), k).start()

    def expect(zi, xi):
        mine = at(zi, xi, c)

        @pl.when(mine != me)
        def _():
            i_arrival(at(zi, xi, 0), 2).wait_recv()

        @pl.when(mine == me)
        def _():
            i_arrival(at(zi, xi, 0), 1).wait_recv()

        return mine

    def core_slot(zi, xi):
        slot = at(zi, xi, other)
        ref = gat.at[slot]
        rcopy(ref, ref, ac_s, gc_r.at[zi * nx + xi], {"tbl": at(z, x, other)}).wait_recv()
        return slot

    def pair_proc(zi, xi):
        mine = expect(zi, xi)
        proc(mine, core_slot(zi, xi))

    zr = nz - 1 - z

    def step_body(i, carry):
        j = i // PIECES + 1
        k = lax.rem(i, PIECES)
        s = j - 1

        @pl.when(z - j >= 0)
        def _():
            from_z(z - j, k, z + 1 < nz, right_copy)

        @pl.when(z + j < nz)
        def _():
            from_z(z + j, k, z >= 1, left_copy)

        from_x(i)

        @pl.when((s <= nz - 2) & (z >= 1) & (z <= s))
        def _():
            t = nz - 1 - s + z
            rin_copy(t, k).wait_recv()
            chain_step(t, k, rin, rin_copy)

        @pl.when((s <= nz - 2) & (zr >= 1) & (zr <= s))
        def _():
            t = s - zr
            lin_arrival(t, k).wait_recv()
            chain_step(t, k, lin, lin_copy)

        @pl.when(s == nz - 1)
        def _():
            finish_cut(k)

        @pl.when(i == 1)
        def _():
            chain_heads()
            prepare_inverse()

        @pl.when(i == 2)
        def _():
            prepare_wide()

        @pl.when(i == 3)
        def _():
            prepare_evict()

        @pl.when(i == 2 * PIECES - 1)
        def _():
            inv_copy.wait()
            src_copy.wait()
            prepare_fetch(0, nh * cap // 16)

        @pl.when(i == 3 * PIECES - 1)
        def _():
            prepare_fetch(nh * cap // 16, nh * cap // 8)

        side = lax.rem(k, 2) == 0
        near = k < 2
        end = s == nz - 1
        below = z - s
        line = jnp.where(side & ((below >= 0) | ~end), below, z + s)
        near = near & (side | ((s >= 1) & ~end))
        zi = jnp.where(near, line, ring(jnp.maximum(s - 1, 0)))
        on_line = near & (zi >= 0) & (zi < nz)
        on_side = (k == jnp.where(end, 1, 2)) & (s >= 1)

        @pl.when(on_line | on_side)
        def _():
            def one(dx, carry):
                pair_proc(zi, xof(dx))
                return carry

            lax.fori_loop(jnp.where(near, 0, 1), jnp.where(near, 1, nx), one, 0)

        return carry

    lax.fori_loop(0, PIECES * nz, step_body, 0)
    for dx in range(1, nx):
        proc(expect(ring(nz - 1), xof(dx)))
        proc(core_slot(ring(nz - 1), xof(dx)))

    def gathered(first):
        picks = []
        for q in range(8):
            picks.append(place[pl.ds(first(q), 1), :])
        return jnp.concatenate(picks, axis=0)

    step = 64

    def ev_gather(i, carry):
        k = i // (cap // step)
        p = lax.rem(i, cap // step) * step
        for b in range(0, step, 8):
            ev_g[k, pl.ds(pl.multiple_of(p + b, 8), 8), :] = gathered(
                lambda q: ev_s[k, p + b + q]
            )
        return carry

    lax.fori_loop(0, nh * cap // step, ev_gather, 0)

    def er_copy(d, slot):
        k = lax.rem(h + d, nh)
        return rcopy(ev_half.at[k], half_in.at[slot], er_s, er_r.at[slot], {"hst": k})

    def ea_copy(d, slot):
        k = lax.rem(h + d, nh)
        return rcopy(ev_acc.at[k], acc_in.at[slot], ea_s, ea_r.at[slot], {"hst": k})

    for d in range(1, nh + 1):
        k = lax.rem(h + d, nh)
        for r0 in range(0, cap, emb):
            span_k = pl.ds(r0, emb)
            g = ev_g[k, span_k]
            acc = ev_a[k, span_k] + jnp.mean(g * g, axis=1, keepdims=True)
            ev_rows[k, span_k] = ev_w[k, span_k] - LEARN_RATE * g / (jnp.sqrt(acc) + EPSILON)
            ev_acc[k, :, span_k] = jnp.sum(jnp.where(eye, acc, 0.0), axis=0, keepdims=True)
        if d < nh:
            ev_half[k] = ev_rows[k].astype(BF16)
            er_copy(d, h).start()
            ea_copy(d, h).start()
    def held_out(buf, acc, k):
        return (
            pltpu.make_async_copy(buf.at[k], held_rows_o.at[k], out_s.at[2 + k]),
            pltpu.make_async_copy(acc.at[k], held_accum_o.at[k], out_s.at[2 + nh + k]),
        )

    for copy in held_out(ev_rows, ev_acc, h):
        copy.start()

    batch_tiles = max(u for u in (1, 2, UPDATE_TILES) if groups % u == 0)
    spread = batch_tiles * emb

    def weight_out(i):
        at_i = pl.ds(pl.multiple_of(i * spread, spread), spread)
        return pltpu.make_async_copy(new_weight.at[at_i], new_weight_o.at[at_i], w_s)

    def update(i2, carry):
        for u in range(batch_tiles):
            i = i2 * batch_tiles + u
            total = jnp.zeros((8, emb), F32)
            for b in range(emb // 8):
                rows_b = pl.ds(pl.multiple_of(i * emb + b * 8, 8), 8)
                g = gathered(lambda q: inv_s[i, b * 8 + q])
                acc = wide[rows_b, :] + jnp.mean(g * g, axis=1, keepdims=True)
                new_weight[rows_b, :] = weight_v[rows_b, :] - LEARN_RATE * g / (
                    jnp.sqrt(acc) + EPSILON
                )
                diag = iota((8, emb), 1) == iota((8, emb), 0) + b * 8
                total = total + jnp.where(diag, acc, 0.0)
            new_accum[pl.ds(i, 1), :] = jnp.sum(total, axis=0, keepdims=True)
        weight_out(i2).start()
        return carry

    lax.fori_loop(0, groups // batch_tiles, update, 0)
    accum_out = pltpu.make_async_copy(new_accum, new_accum_o, out_s.at[0])
    accum_out.start()

    for d in range(1, nx):
        xs_arrival(d).wait_recv()
    for j in range(CUTS):
        s = own_sum(z, j, x)
        for d in range(1, nx):
            s = s + xr[xof(d), j].astype(F32)
        grad_up[:, cutcols(j)] = s
    grad_out_copy = pltpu.make_async_copy(grad_up, grad_up_o, out_s.at[1])
    grad_out_copy.start()

    for d in range(1, nh):
        k = lax.rem(h + d, nh)
        er_copy(d, k).wait_recv()
        ea_copy(d, k).wait_recv()
        rows_in[k] = half_in[k].astype(F32)
        for copy in held_out(rows_in, acc_in, k):
            copy.start()

    def all_sent(ref, sem, recv, dev):
        rcopy(ref, ref, sem, recv, dev).wait_send()

    core_dev = {"tbl": at(z, x, other)}
    if nh > 1:
        host_dev = {"hst": lax.rem(h + 1, nh)}
        all_sent(ev_half.at[pl.ds(0, nh - 1)], er_s, er_r.at[0], host_dev)
        all_sent(ev_acc.at[pl.ds(0, nh - 1)], ea_s, ea_r.at[0], host_dev)
        all_sent(fsend, y_s, y_r.at[0, 0], host_dev)
    all_sent(rcore, rc_s, rc_r, core_dev)
    all_sent(idx.at[pl.ds(0, n - 1)], i_s, i_r.at[0], core_dev)
    all_sent(gat.at[pl.ds(0, nz * nx)], ac_s, gc_r.at[0], core_dev)
    if nx > 1:
        all_sent(xs, xs_s, xr_r.at[0], core_dev)
        all_sent(gat.at[pl.ds(0, nz * (nx - 1))], ax_s, gc_r.at[0], core_dev)
    if nz > 1:
        all_sent(chain.at[pl.ds(0, nz - 1)], ch_s, ci_r.at[0, 0], core_dev)
    for q in range(nz - 1):

        @pl.when(z == q)
        def _(q=q):
            all_sent(gat.at[pl.ds(0, q + 1)], azr_s, gc_r.at[0], core_dev)

        @pl.when(zr == q)
        def _(q=q):
            all_sent(gat.at[pl.ds(0, q + 1)], azl_s, gc_r.at[0], core_dev)

    pltpu.make_async_copy(new_weight, new_weight_o, w_s).wait()
    accum_out.wait()
    grad_out_copy.wait()
    for d in range(nh):
        k = lax.rem(h + d, nh)
        buf, acc = (ev_rows, ev_acc) if d == 0 else (rows_in, acc_in)
        for copy in held_out(buf, acc, k):
            copy.wait()


def write_kernel(*refs):
    sems = refs[10]
    copies = [pltpu.make_async_copy(refs[k], refs[5 + k], sems.at[k]) for k in range(5)]
    for copy in copies:
        copy.start()
    for copy in copies:
        copy.wait()


def on_device(
    nz, nx,
    pooled, w_up, grad_out, owners, rows, lookup_weight, lens, slot_map,
    cache_weight, cache_accum, evict_slots, evict_dest, evict_count,
):
    tables, batch, bag = owners.shape
    slots = slot_map.shape[-1]
    rows_dev = slots // tables
    emb = cache_weight.shape[-1]
    n = lax.axis_size("tbl")
    nh = lax.axis_size("hst")
    feat_n, hid = w_up.shape
    out_rows = feat_n // n
    width = tables * emb
    groups = slots // emb
    list_len = evict_slots.shape[-1]
    cap = list_len // 2
    cut = hid // CUTS
    tile = min(512, hid)

    dma = pltpu.SemaphoreType.DMA
    anyspace = pl.BlockSpec(memory_space=pltpu.HBM)
    i32 = jnp.int32
    grad_up, new_weight, new_accum, held_rows, held_accum = pl.pallas_call(
        functools.partial(step_kernel, nz, nx, nh, tables, rows_dev, tile),
        out_shape=(
            jax.ShapeDtypeStruct((out_rows, hid), F32),
            jax.ShapeDtypeStruct((slots, emb), F32),
            jax.ShapeDtypeStruct((groups, emb), F32),
            jax.ShapeDtypeStruct((nh, cap, emb), F32),
            jax.ShapeDtypeStruct((nh, 1, cap), F32),
        ),
        in_specs=[anyspace] * 12 + [pl.BlockSpec(memory_space=pltpu.SMEM)],
        out_specs=(pl.BlockSpec(memory_space=pl.ANY),) * 5,
        scratch_shapes=[
            pltpu.VMEM((out_rows, hid), F32),
            pltpu.VMEM((slots, emb), F32),
            pltpu.VMEM((groups, emb), F32),
            pltpu.VMEM((batch, feat_n), BF16),
            pltpu.VMEM((feat_n, batch), BF16),
            pltpu.VMEM((feat_n, hid), BF16),
            pltpu.VMEM((batch, hid), BF16),
            pltpu.VMEM((batch, hid), BF16),
            pltpu.VMEM((tables, bag, batch), i32),
            pltpu.VMEM((tables, bag, batch), i32),
            pltpu.VMEM((tables, bag, batch), BF16),
            pltpu.VMEM((tables, batch), i32),
            pltpu.VMEM((1, slots), i32),
            pltpu.VMEM((slots, emb), F32),
            pltpu.VMEM((groups, emb), F32),
            pltpu.VMEM((1, list_len), i32),
            pltpu.VMEM((1, list_len), i32),
            pltpu.VMEM((batch, width), F32),
            pltpu.VMEM((nh - 1, batch, width), BF16),
            pltpu.VMEM((nh, batch, width), BF16),
            pltpu.VMEM((n, batch, width), BF16),
            pltpu.VMEM((n, tables, batch), F32),
            pltpu.VMEM((n, tables, batch), F32),
            pltpu.VMEM((CUTS, nz, nx, 2, out_rows, cut), F32),
            pltpu.VMEM((CUTS, nz, nx, out_rows, cut), F32),
            pltpu.VMEM((nz, CUTS, nx, out_rows, cut), BF16),
            pltpu.VMEM((nz, CUTS, nx, out_rows, cut), BF16),
            pltpu.VMEM((nz, CUTS, nx, out_rows, cut), BF16),
            pltpu.VMEM((max(nx - 1, 1), CUTS, out_rows, cut), BF16),
            pltpu.VMEM((nx, CUTS, out_rows, cut), BF16),
            pltpu.VMEM((slots + 8, emb), F32),
            pltpu.VMEM((slots, emb), F32),
            pltpu.VMEM((groups, emb), i32),
            pltpu.VMEM((nh, cap), i32),
            pltpu.SMEM((groups, emb), i32),
            pltpu.SMEM((nh, cap), i32),
            pltpu.SMEM((nh, cap), i32),
            pltpu.VMEM((nh, cap, emb), F32),
            pltpu.VMEM((nh, cap, emb), F32),
            pltpu.VMEM((nh, cap, emb), F32),
            pltpu.VMEM((nh, cap, emb), F32),
            pltpu.VMEM((nh, 1, cap), F32),
            pltpu.VMEM((nh, cap, emb), F32),
            pltpu.VMEM((nh, 1, cap), F32),
            pltpu.VMEM((nh, cap, emb), BF16),
            pltpu.VMEM((nh, cap, emb), BF16),
            dma((1 + hid // tile + BLOCKS + 9,)), dma((2,)),
            dma, dma((max(nh - 1, 1), PIECES)), dma, dma((nz * nx,)),
            dma, dma, dma, dma, dma((nz * nx, PIECES)), dma((nz * nx,)), dma, dma,
            dma, dma((nz + 1, CUTS)), dma, dma((max(nx - 1, 1),)),
            dma, dma((nh,)), dma, dma((nh,)), dma((2 + 2 * nh,)), dma,
        ],
        compiler_params=pltpu.CompilerParams(
            collective_id=0, has_side_effects=True, vmem_limit_bytes=48 * 1024 * 1024
        ),
        name="step",
    )(*[pltpu.with_memory_space_constraint(v, pltpu.HBM) for v in (
        pooled, w_up, grad_out,
        jnp.transpose(owners, (0, 2, 1)), jnp.transpose(rows, (0, 2, 1)),
        jnp.transpose(lookup_weight, (0, 2, 1)), lens, slot_map.reshape(1, slots),
        cache_weight.reshape(slots, emb), cache_accum.reshape(groups, emb),
        evict_slots.reshape(1, list_len), evict_dest.reshape(1, list_len),
    )], evict_count)
    outs = (grad_up, new_weight, new_accum, held_rows, held_accum)
    hbm = pl.BlockSpec(memory_space=pltpu.HBM)
    grad_up, new_weight, new_accum, held_rows, held_accum = pl.pallas_call(
        write_kernel,
        out_shape=tuple(jax.ShapeDtypeStruct(v.shape, v.dtype) for v in outs),
        in_specs=[pl.BlockSpec(memory_space=pl.ANY)] * 5,
        out_specs=(hbm,) * 5,
        scratch_shapes=[dma((5,))],
        compiler_params=pltpu.CompilerParams(vmem_limit_bytes=1024 * 1024),
        name="write",
    )(*outs)
    return (
        grad_up,
        new_weight[None, None],
        new_accum.reshape(1, 1, slots),
        held_rows[None, None],
        held_accum.reshape(1, 1, nh, cap),
    )


def solution(mesh):
    n, nh = mesh.shape["tbl"], mesh.shape["hst"]
    nx = nh if n % (2 * nh) == 0 else 1
    nz = n // (2 * nx)
    placed = (
        P("tbl", None),
        P(None, "hst"),
        P("tbl", "hst"),
        P("hst", "tbl", None),
        P("hst", "tbl", None),
        P("hst", "tbl", None),
        P("hst", "tbl"),
        P("tbl", "hst", None),
        P("tbl", "hst", None, None),
        P("tbl", "hst", None),
        P("tbl", "hst", None),
        P("tbl", "hst", None),
        P("tbl", "hst"),
    )
    return jax.shard_map(
        functools.partial(on_device, nz, nx),
        mesh=mesh,
        in_specs=placed,
        out_specs=(
            P("tbl", "hst"),
            P("tbl", "hst", None, None),
            P("tbl", "hst", None),
            P("tbl", "hst", None, None, None),
            P("tbl", "hst", None, None),
        ),
        check_vma=False,
    )
```

```python
import functools

import jax
import jax.numpy as jnp
from jax import lax
from jax.experimental import pallas as pl
from jax.experimental.pallas import tpu as pltpu
from jax.sharding import PartitionSpec as P

LEARN_RATE = 0.05
EPSILON = 1e-08
MESH = pl.DeviceIdType.MESH
BLOCKS = 2
SUBS = 2
PIECES = BLOCKS * SUBS
CUTS = 4
UPDATE_TILES = 4
RADIX = 256
ROW_STEP = 2048.0
WEIGHT_STEP = 512.0
F32 = jnp.float32
BF16 = jnp.bfloat16
NT_DIMS = (((1,), (1,)), ((), ()))


def iota(shape, axis):
    return lax.broadcasted_iota(jnp.int32, shape, axis)


def step_kernel(
    nz, nx, nh, tables, rows_dev, tile,
    pooled, w_up, grad_out, owners, rows, lookup_weight, lens, slot_map,
    weight, accum, evict_slots, evict_dest, evict_count,
    grad_up_o, new_weight_o, new_accum_o, held_rows_o, held_accum_o,
    grad_up, new_weight, new_accum, pooled_v, pooled_t, w_v, go_v, delta, own_v, row_v, lw_v, len_v, map_v, weight_v, accum_v,
    es_v, ed_v,
    fown, fsend, ybuf, gat, idx, idxb, grad, rcore, chain, rin, lin, xs, xr, place,
    wide, inv_v, src_v, ev_v, inv_s, src_s, ev_s, ev_w, ev_a, ev_g, ev_rows, ev_acc, rows_in, acc_in, ev_half, half_in, ev_ok,
    ld_s, sm_s, y_s, y_r, i_s, i_r, azr_s, azl_s, ax_s, ac_s, g_r, gc_r, rc_s, rc_r,
    ch_s, ci_r, xs_s, xr_r, er_s, er_r, ea_s, ea_r, out_s, w_s,
):
    n = nz * nx * 2
    me = lax.axis_index("tbl")
    h = lax.axis_index("hst")
    c = lax.rem(me, 2)
    zx = me // 2
    x = lax.rem(zx, nx)
    z = zx // nx
    other = 1 - c
    batch, hid = grad_out.shape
    feat_n = pooled.shape[1]
    width = ybuf.shape[-1]
    emb = width // tables
    bag = owners.shape[1]
    slots = weight.shape[0]
    list_len = evict_slots.shape[1]
    cap = ev_rows.shape[1]
    out_rows = grad.shape[4]
    cut = hid // CUTS
    piece = batch // PIECES
    block = batch // BLOCKS
    tiles = hid // tile

    def at(zi, xi, ci):
        return (zi * nx + xi) * 2 + ci

    def xof(d):
        return lax.rem(x + d, nx)

    def rcopy(src, dst, s, r, dev):
        return pltpu.make_async_remote_copy(
            src_ref=src, dst_ref=dst, send_sem=s, recv_sem=r,
            device_id=dev, device_id_type=MESH,
        )

    def cols(hh):
        return pl.ds(pl.multiple_of(hh * width, width), width)

    def span(k):
        return pl.ds(k * piece, piece)

    def spanb(k):
        return pl.ds(k * block, block)

    def cutcols(j):
        return pl.ds(j * cut, cut)

    def tilecols(j):
        return pl.ds(j * tile, tile)

    p_loads = [
        pltpu.make_async_copy(pooled.at[spanb(k)], pooled_v.at[spanb(k)], ld_s.at[k])
        for k in range(BLOCKS)
    ]
    base = BLOCKS
    w_loads = [
        pltpu.make_async_copy(w_up.at[:, tilecols(j)], w_v.at[:, tilecols(j)], ld_s.at[base + j])
        for j in range(tiles)
    ]
    base = base + tiles
    g_first = [
        pltpu.make_async_copy(
            grad_out.at[spanb(0), tilecols(j)], go_v.at[spanb(0), tilecols(j)], ld_s.at[base + j]
        )
        for j in range(tiles)
    ]
    base = base + tiles
    g_loads = [
        pltpu.make_async_copy(grad_out.at[spanb(k)], go_v.at[spanb(k)], ld_s.at[base + k - 1])
        for k in range(1, BLOCKS)
    ]
    base = base + BLOCKS - 1
    small = [
        pltpu.make_async_copy(src, dst, ld_s.at[base + k])
        for k, (src, dst) in enumerate((
            (owners, own_v), (rows, row_v), (lookup_weight, lw_v), (lens, len_v),
            (slot_map, map_v), (evict_slots, es_v), (evict_dest, ed_v),
            (accum, accum_v), (weight, weight_v),
        ))
    ]
    p_loads[0].start()
    w_loads[0].start()
    g_first[0].start()
    barrier = pltpu.get_barrier_semaphore()

    def greet(d, carry):
        pl.semaphore_signal(
            barrier, inc=1, device_id={"tbl": lax.rem(me + d, n)}, device_id_type=MESH
        )
        return carry

    lax.fori_loop(1, n, greet, 0)
    for d in range(1, nh):
        pl.semaphore_signal(
            barrier, inc=1, device_id={"hst": lax.rem(h + d, nh)}, device_id_type=MESH
        )
    for j in range(1, tiles):
        w_loads[j].start()
        g_first[j].start()
    for copy in p_loads[1:] + small + g_loads:
        copy.start()

    def y_copy(d, k):
        h2 = lax.rem(h + d, nh)
        return rcopy(
            fsend.at[d - 1, span(k)], ybuf.at[h, span(k)], y_s, y_r.at[nh - d - 1, k], {"hst": h2}
        )

    def y_arrival(d, k):
        h2 = lax.rem(h + d, nh)
        return rcopy(
            fsend.at[d - 1, span(k)], ybuf.at[h2, span(k)], y_s, y_r.at[d - 1, k],
            {"hst": h2},
        )

    def deltas(k):
        p_loads[k].wait()
        if k > 0:
            g_loads[k - 1].wait()
        for j in range(tiles):
            if k == 0:
                w_loads[j].wait()
                g_first[j].wait()
            cs = pl.ds(j * tile, tile)
            p = jnp.dot(pooled_v[spanb(k), :], w_v[:, cs], preferred_element_type=F32)
            s = jax.nn.sigmoid(p)
            g = go_v[spanb(k), cs].astype(F32)
            delta[spanb(k), cs] = (g * s * (1.0 + p * (1.0 - s))).astype(BF16)

    def feats_out(k):
        for d in range(1, nh):
            h2 = lax.rem(h + d, nh)
            part = lax.dot_general(
                delta[spanb(k), :], w_v[cols(h2), :], NT_DIMS, preferred_element_type=F32
            )
            fsend[d - 1, spanb(k)] = part.astype(BF16)
            if k == 0 and d == 1:
                pl.semaphore_wait(barrier, n - 1 + nh - 1)
            y_copy(d, k * SUBS).start()

    def feats_rest(k):
        for q in range(1, SUBS):
            for d in range(1, nh):
                y_copy(d, k * SUBS + q).start()

    def feats_own(k):
        fown[spanb(k), :] = lax.dot_general(
            delta[spanb(k), :], w_v[cols(h), :], NT_DIMS, preferred_element_type=F32
        )

    def i_copy(d):
        o = lax.rem(me + d, n)
        return rcopy(idx.at[o], idxb.at[me], i_s, i_r.at[zx], {"tbl": o})

    def i_arrival(first, count):
        ref = idxb.at[pl.ds(first, count)]
        return rcopy(ref, ref, i_s, i_r.at[first // 2], {"tbl": at(z, x, other)})


    def g_copy(slot, k, sem, dev):
        ref = gat.at[slot, span(k)]
        return rcopy(ref, ref, sem, g_r.at[slot // 2, k], {"tbl": dev})


    def right_copy(zi, k):
        return g_copy(at(zi, x, c), k, azr_s, at(z + 1, x, c))

    def left_copy(zi, k):
        return g_copy(at(zi, x, c), k, azl_s, at(z - 1, x, c))

    def x_copy(zi, d, k):
        return g_copy(at(zi, x, c), k, ax_s, at(z, xof(d), c))

    both = jnp.minimum(z, nz - 1 - z)

    def ring(e):
        dist = (e + 1) // 2
        near = jnp.where(lax.rem(e, 2) == 1, z - dist, z + dist)
        dist = e - both
        far = jnp.where(z - dist >= 0, z - dist, z + dist)
        return jnp.where(e <= 2 * both, near, far)

    def c_copy(zi, xi, k):
        ref = gat.at[at(zi, xi, c), span(k)]
        late = (zi == ring(nz - 1)) & (xi != x)
        spot = jnp.where(late, nz * nx + 2 * xi + k // (PIECES // 2), zi * nx + xi)
        return rcopy(ref, ref, ac_s, gc_r.at[spot], {"tbl": at(z, x, other)})

    def arrived(slot, k):
        g_copy(slot, k, ac_s, at(z, x, other)).wait_recv()

    def gather_start(k):
        total = fown[span(k), :]
        for d in range(1, nh):
            y_arrival(d, k).wait_recv()
            total = total + ybuf[lax.rem(h + d, nh), span(k)].astype(F32)
        gat[me, span(k)] = total.astype(BF16)

        @pl.when(z + 1 < nz)
        def _():
            right_copy(z, k).start()

        @pl.when(z >= 1)
        def _():
            left_copy(z, k).start()

        for d in range(1, nx):
            x_copy(z, d, k).start()
        c_copy(z, x, k).start()

    def core_copy(j):
        return rcopy(
            grad.at[j, :, :, other], rcore.at[j], rc_s, rc_r, {"tbl": at(z, x, other)}
        )

    def weight_grad(j):
        part = jnp.dot(pooled_t[...], delta[:, cutcols(j)], preferred_element_type=F32)
        grad[j] = part.reshape(nz, nx, 2, out_rows, cut)
        core_copy(j).start()

    deltas(0)
    feats_out(0)
    for copy in small:
        copy.wait()
    for t in range(tables):
        used = iota((bag, batch), 0) < len_v[t : t + 1, :]
        code = (row_v[t] + 1).astype(F32) * ROW_STEP + lw_v[t].astype(F32) * WEIGHT_STEP
        code = jnp.where(used, code, 0.0)
        for o in range(n):
            idx[o, t : t + 1, :] = jnp.sum(
                jnp.where(own_v[t] == o, code, 0.0), axis=0, keepdims=True
            )
    idxb[me] = idx[me]

    def i_start(d, carry):
        i_copy(d).start()
        return carry

    lax.fori_loop(1, n, i_start, 0)

    feats_own(0)
    feats_rest(0)
    deltas(1)
    feats_out(1)
    feats_rest(1)
    gather_start(0)
    feats_own(1)
    pooled_t[...] = pooled_v[...].T
    weight_grad(0)
    for k in range(1, PIECES):
        gather_start(k)
        weight_grad(k)

    place[...] = jnp.zeros_like(place)
    chunk = min(RADIX, rows_dev)

    def proc(*picked, rows_of=slice(0, batch)):
        codes = [idxb[slot][:, rows_of] for slot in picked]
        count = rows_of.stop - rows_of.start
        bags = [gat[slot, pl.ds(rows_of.start, count), :] for slot in picked]
        for t in range(tables):
            pairs = []
            for code, bag_rows in zip(codes, bags):
                code = code[t : t + 1, :]
                row1 = jnp.floor(code * (1.0 / ROW_STEP))
                wgt = ((code - row1 * ROW_STEP) * (1.0 / WEIGHT_STEP)).astype(BF16)
                pairs.append((row1 - 1.0, wgt, bag_rows[:, t * emb : (t + 1) * emb]))
            ids = iota((chunk, count), 0).astype(F32).astype(BF16)
            for r0 in range(0, rows_dev, chunk):
                total = None
                for row, wgt, part in pairs:
                    near = row - float(r0)
                    near = jnp.where((near >= 0.0) & (near < float(chunk)), near, -1.0)
                    mark = jnp.where(ids == near.astype(BF16), wgt, jnp.zeros((), BF16))
                    prod = jnp.dot(mark, part, preferred_element_type=F32)
                    total = prod if total is None else total + prod
                place[pl.ds(t * rows_dev + r0, chunk), :] += total

    eye = iota((emb, emb), 0) == iota((emb, emb), 1)
    groups = slots // emb

    inv_copy = pltpu.make_async_copy(inv_v, inv_s, sm_s.at[0])
    src_copy = pltpu.make_async_copy(src_v, src_s, sm_s.at[1])
    ev_copy = pltpu.make_async_copy(ev_v, ev_s, sm_s.at[2])

    def prepare_inverse():
        home = map_v[...].astype(F32)
        high = jnp.floor(home * (1.0 / emb))
        low = home - high * emb
        from_row = iota((1, slots), 1).astype(F32)
        from_high = jnp.floor(from_row * (1.0 / RADIX))
        from_low = from_row - from_high * RADIX
        in_group = iota((groups, slots), 0).astype(F32) == high
        left = jnp.concatenate(
            [jnp.where(in_group, from_high, 0.0), jnp.where(in_group, from_low, 0.0)], axis=0
        ).astype(BF16)
        right = jnp.where(iota((emb, slots), 0).astype(F32) == low, 1.0, 0.0).astype(BF16)
        found = lax.dot_general(left, right, NT_DIMS, preferred_element_type=F32)
        inv = (found[:groups] * RADIX + found[groups:]).astype(jnp.int32)
        inv_v[...] = jnp.clip(inv, 0, slots - 1)
        inv_copy.start()
        return found.astype(BF16)


    def prepare_wide():
        for i in range(groups):
            col = jnp.sum(jnp.where(eye, accum_v[i : i + 1, :], 0.0), axis=1, keepdims=True)
            wide[i * emb : (i + 1) * emb, :] = jnp.broadcast_to(col, (emb, emb))

    def prepare_evict(found):
        live = iota((1, list_len), 1) < evict_count[0, 0]
        lanes = 8 * -(-nh // 8)
        mine = jnp.where((iota((lanes, list_len), 0) == ed_v[...]) & live, 1.0, 0.0)
        before = jnp.where(iota((list_len, list_len), 0) < iota((list_len, list_len), 1), 1.0, 0.0)
        goal = jnp.dot(mine.astype(BF16), before.astype(BF16), preferred_element_type=F32)
        slot1 = es_v[...].astype(F32)
        slot_high = jnp.floor(slot1 * (1.0 / RADIX))
        slot_low = slot1 - slot_high * RADIX
        parts = jnp.where(iota((8, list_len), 0) == 0, slot_high, slot_low).astype(BF16)
        for d in range(nh):
            hot = jnp.where(
                iota((cap, list_len), 0).astype(F32) == goal[d : d + 1], mine[d : d + 1], 0.0
            )
            ev_ok[d] = jnp.broadcast_to(jnp.sum(hot, axis=1, keepdims=True), (cap, emb))
            hot = hot.astype(BF16)
            got = lax.dot_general(parts, hot, NT_DIMS, preferred_element_type=F32)
            src = (got[0:1] * RADIX + got[1:2]).astype(jnp.int32)
            src_v[d : d + 1, :] = jnp.clip(src, 0, slots - 1)
            from_slot = got[0:1] * RADIX + got[1:2]
            slot_group = jnp.floor(from_slot * (1.0 / emb))
            slot_lane = from_slot - slot_group * emb
            lane_hot = jnp.where(iota((emb, cap), 0).astype(F32) == slot_lane, 1.0, 0.0)
            taken = jnp.dot(found, lane_hot.astype(BF16), preferred_element_type=F32)
            in_slot_group = iota((groups, cap), 0).astype(F32) == slot_group
            row_high = jnp.sum(jnp.where(in_slot_group, taken[:groups], 0.0), axis=0, keepdims=True)
            row_low = jnp.sum(jnp.where(in_slot_group, taken[groups:], 0.0), axis=0, keepdims=True)
            ev_row = (row_high * RADIX + row_low).astype(jnp.int32)
            ev_v[d : d + 1, :] = jnp.clip(ev_row, 0, slots - 1)
        src_copy.start()
        ev_copy.start()


    def gathered(ref, index):
        return jnp.concatenate([ref[pl.ds(index(q), 1), :] for q in range(8)], axis=0)

    unroll = 64

    def each_evicted(body):
        def trip(i, carry):
            k = i // (cap // unroll)
            p = lax.rem(i, cap // unroll) * unroll
            for b in range(0, unroll, 8):
                body(k, p + b, pl.ds(pl.multiple_of(p + b, 8), 8))
            return carry

        lax.fori_loop(0, nh * cap // unroll, trip, 0)

    def prepare_fetch():
        def fetch(k, p, rows_p):
            ev_w[k, rows_p, :] = gathered(weight_v, lambda q: src_s[k, p + q])
            ev_a[k, rows_p, :] = gathered(wide, lambda q: src_s[k, p + q])

        each_evicted(fetch)

    def rin_copy(t, j):
        return rcopy(
            chain.at[t, j], rin.at[t, j], ch_s, ci_r.at[t, j], {"tbl": at(z + 1, x, c)}
        )

    def lin_copy(t, j):
        return rcopy(
            chain.at[t, j], lin.at[t, j], ch_s, ci_r.at[jnp.where(t == z - 1, nz, t), j],
            {"tbl": at(z - 1, x, c)},
        )

    def lin_arrival(t, j):
        return rcopy(
            chain.at[t, j], lin.at[t, j], ch_s, ci_r.at[jnp.where(t == z, nz, t), j],
            {"tbl": at(z - 1, x, c)},
        )

    def own_sum(t, j, xi):
        return grad[j, t, xi, c] + rcore[j, t, xi]

    def chain_step(t, j, buf, copy):
        for xi in range(nx):
            s = own_sum(t, j, xi)
            if buf is not None:
                s = s + buf[t, j, xi].astype(F32)
            chain[t, j, xi] = s.astype(BF16)
        copy(t, j).start()


    def chain_heads():
        rcopy(rcore, rcore, rc_s, rc_r, {"tbl": at(z, x, other)}).wait_recv()

        @pl.when(z == 0)
        def _():
            def body(i, carry):
                for j in range(CUTS):
                    chain_step(nz - 1 - i, j, None, rin_copy)
                return carry

            lax.fori_loop(0, nz - 1, body, 0)

        @pl.when(z == nz - 1)
        def _():
            def body(i, carry):
                for j in range(CUTS):
                    chain_step(i, j, None, lin_copy)
                return carry

            lax.fori_loop(0, nz - 1, body, 0)

    def xs_copy(d, j):
        x2 = xof(d)
        return rcopy(xs.at[d - 1, j], xr.at[x, j], xs_s, xr_r.at[nx - d - 1], {"tbl": at(z, x2, c)})

    def xs_arrival(d):
        x2 = xof(d)
        return rcopy(xs.at[d - 1], xr.at[x2], xs_s, xr_r.at[d - 1], {"tbl": at(z, x2, c)})

    def finish_cut(j):
        @pl.when(z >= 1)
        def _():
            rin_copy(z, j).wait_recv()
            for xi in range(nx):
                grad[j, z, xi, c] += rin[z, j, xi].astype(F32)

        @pl.when(z + 1 < nz)
        def _():
            lin_arrival(z, j).wait_recv()
            for xi in range(nx):
                grad[j, z, xi, c] += lin[z, j, xi].astype(F32)

        for d in range(1, nx):
            xs[d - 1, j] = own_sum(z, j, xof(d)).astype(BF16)
            xs_copy(d, j).start()

    def from_z(zi, k, open_end, onward):
        arrived(at(zi, x, c), k)

        @pl.when(open_end)
        def _():
            onward(zi, k).start()

        for dx in range(1, nx):
            x_copy(zi, dx, k).start()
        c_copy(zi, x, k).start()

    def from_x(i):
        head = i < PIECES
        i2 = i - PIECES
        paired = i2 < 2 * PIECES * both
        r = lax.rem(i2, 2 * PIECES)
        i3 = i2 - 2 * PIECES * both
        e = jnp.where(
            head, 0,
            jnp.where(
                paired, 1 + 2 * (i2 // (2 * PIECES)) + lax.rem(r, 2), 1 + 2 * both + i3 // PIECES
            ),
        )
        k = jnp.where(head, i, jnp.where(paired, r // 2, lax.rem(i3, PIECES)))
        zi = ring(e)
        for dx in range(1, nx):
            arrived(at(zi, xof(dx), c), k)
            c_copy(zi, xof(dx), k).start()

    def expect(zi, xi):
        mine = at(zi, xi, c)

        @pl.when(mine != me)
        def _():
            i_arrival(at(zi, xi, 0), 2).wait_recv()

        @pl.when(mine == me)
        def _():
            i_arrival(at(zi, xi, 0), 1).wait_recv()

        return mine

    def core_slot(zi, xi):
        slot = at(zi, xi, other)
        ref = gat.at[slot]
        rcopy(ref, ref, ac_s, gc_r.at[zi * nx + xi], {"tbl": at(z, x, other)}).wait_recv()
        return slot

    halves = [slice(0, batch // 2), slice(batch // 2, batch)]
    final = ring(nz - 1)

    def core_half(xi, q):
        slot = at(final, xi, other)
        ref = gat.at[slot, pl.ds(q * (batch // 2), batch // 2)]
        core = {"tbl": at(z, x, other)}
        rcopy(ref, ref, ac_s, gc_r.at[nz * nx + 2 * xi + q], core).wait_recv()
        return slot

    def pair_proc(zi, xi):
        mine = expect(zi, xi)
        proc(mine, core_slot(zi, xi))

    zr = nz - 1 - z

    def step_body(i, carry):
        j = i // PIECES + 1
        k = lax.rem(i, PIECES)
        s = j - 1

        @pl.when(z - j >= 0)
        def _():
            from_z(z - j, k, z + 1 < nz, right_copy)

        @pl.when(z + j < nz)
        def _():
            from_z(z + j, k, z >= 1, left_copy)

        from_x(i)

        @pl.when((s <= nz - 2) & (z >= 1) & (z <= s))
        def _():
            t = nz - 1 - s + z
            rin_copy(t, k).wait_recv()
            chain_step(t, k, rin, rin_copy)

        @pl.when((s <= nz - 2) & (zr >= 1) & (zr <= s))
        def _():
            t = s - zr
            lin_arrival(t, k).wait_recv()
            chain_step(t, k, lin, lin_copy)

        @pl.when((s == nz - 1) & (k < CUTS - 1))
        def _():
            finish_cut(k)

        @pl.when(i == 0)
        def _():
            found = prepare_inverse()
            prepare_wide()
            prepare_evict(found)

        @pl.when(i == 1)
        def _():
            chain_heads()

        @pl.when(i == 2 * PIECES - 1)
        def _():
            inv_copy.wait()
            src_copy.wait()
            ev_copy.wait()
            prepare_fetch()

        @pl.when(i == PIECES * nz - 2)
        def _():
            def one(dx, carry):
                xi = xof(dx)
                proc(expect(final, xi), core_half(xi, 0), rows_of=halves[0])
                return carry

            lax.fori_loop(1, nx, one, 0)

        side = lax.rem(k, 2) == 0
        near = k < 2
        end = s == nz - 1
        below = z - s
        line = jnp.where(side & ((below >= 0) | ~end) & (s >= 1), below, z + s)
        near = near & ((side & (s >= 1)) | (~side & ~end))
        on_line = near & (line >= 0) & (line < nz)
        zi = jnp.where(on_line, line, ring(jnp.maximum(s - 1, 0)))
        half_pair = (lax.rem(s, 2) == 0) & (s - 1 <= 2 * both)
        at_rim = jnp.where((below >= 0) | (z + s < nz), 1, 0)
        on_side = (k == jnp.where(end, at_rim, jnp.where(half_pair, 3, 2))) & (s >= 1)

        @pl.when(on_line | on_side)
        def _():
            def one(dx, carry):
                pair_proc(zi, xof(dx))
                return carry

            lax.fori_loop(jnp.where(on_line, 0, 1), jnp.where(on_line, 1, nx), one, 0)

        return carry

    lax.fori_loop(0, PIECES * nz, step_body, 0)
    if nx == 1:
        finish_cut(CUTS - 1)
    for dx in range(1, nx):
        proc(at(final, xof(dx), c), rows_of=halves[1])
        if dx == 1:
            finish_cut(CUTS - 1)
        proc(core_half(xof(dx), 1), rows_of=halves[1])

    def ev_gather(k, p, rows_p):
        ev_g[k, rows_p, :] = gathered(place, lambda q: ev_s[k, p + q])

    each_evicted(ev_gather)

    def er_copy(d, slot):
        k = lax.rem(h + d, nh)
        return rcopy(ev_half.at[k], half_in.at[slot], er_s, er_r.at[slot], {"hst": k})

    def ea_copy(d, slot):
        k = lax.rem(h + d, nh)
        return rcopy(ev_acc.at[k], acc_in.at[slot], ea_s, ea_r.at[slot], {"hst": k})

    for d in range(1, nh + 1):
        k = lax.rem(h + d, nh)
        for r0 in range(0, cap, emb):
            span_k = pl.ds(r0, emb)
            g = ev_g[k, span_k]
            acc = ev_a[k, span_k] + jnp.mean(g * g, axis=1, keepdims=True)
            left = ev_w[k, span_k] - LEARN_RATE * g / (jnp.sqrt(acc) + EPSILON)
            used = ev_ok[k, span_k] > 0.5
            ev_rows[k, span_k] = jnp.where(used, left, 0.0)
            ev_acc[k, :, span_k] = jnp.sum(jnp.where(eye & used, acc, 0.0), axis=0, keepdims=True)
        if d < nh:
            ev_half[k] = ev_rows[k].astype(BF16)
            er_copy(d, h).start()
            ea_copy(d, h).start()

    def held_out(buf, acc, k):
        return (
            pltpu.make_async_copy(buf.at[k], held_rows_o.at[k], out_s.at[2 + k]),
            pltpu.make_async_copy(acc.at[k], held_accum_o.at[k], out_s.at[2 + nh + k]),
        )

    for copy in held_out(ev_rows, ev_acc, h):
        copy.start()

    batch_tiles = max(u for u in (1, 2, UPDATE_TILES) if groups % u == 0)
    spread = batch_tiles * emb

    def weight_out(i):
        at_i = pl.ds(pl.multiple_of(i * spread, spread), spread)
        return pltpu.make_async_copy(new_weight.at[at_i], new_weight_o.at[at_i], w_s)

    def update(i2, carry):
        for u in range(batch_tiles):
            i = i2 * batch_tiles + u
            total = jnp.zeros((8, emb), F32)
            for b in range(emb // 8):
                rows_b = pl.ds(pl.multiple_of(i * emb + b * 8, 8), 8)
                g = gathered(place, lambda q: inv_s[i, b * 8 + q])
                acc = wide[rows_b, :] + jnp.mean(g * g, axis=1, keepdims=True)
                new_weight[rows_b, :] = weight_v[rows_b, :] - LEARN_RATE * g / (
                    jnp.sqrt(acc) + EPSILON
                )
                diag = iota((8, emb), 1) == iota((8, emb), 0) + b * 8
                total = total + jnp.where(diag, acc, 0.0)
            new_accum[pl.ds(i, 1), :] = jnp.sum(total, axis=0, keepdims=True)
        weight_out(i2).start()
        return carry

    lax.fori_loop(0, groups // batch_tiles, update, 0)
    accum_out = pltpu.make_async_copy(new_accum, new_accum_o, out_s.at[0])
    accum_out.start()

    for d in range(1, nx):
        xs_arrival(d).wait_recv()
    for j in range(CUTS):
        s = own_sum(z, j, x)
        for d in range(1, nx):
            s = s + xr[xof(d), j].astype(F32)
        grad_up[:, cutcols(j)] = s
    grad_out_copy = pltpu.make_async_copy(grad_up, grad_up_o, out_s.at[1])
    grad_out_copy.start()

    for d in range(1, nh):
        k = lax.rem(h + d, nh)
        er_copy(d, k).wait_recv()
        ea_copy(d, k).wait_recv()
        rows_in[k] = half_in[k].astype(F32)
        for copy in held_out(rows_in, acc_in, k):
            copy.start()

    def all_sent(ref, sem, recv, dev):
        rcopy(ref, ref, sem, recv, dev).wait_send()

    core_dev = {"tbl": at(z, x, other)}
    if nh > 1:
        host_dev = {"hst": lax.rem(h + 1, nh)}
        all_sent(ev_half.at[pl.ds(0, nh - 1)], er_s, er_r.at[0], host_dev)
        all_sent(ev_acc.at[pl.ds(0, nh - 1)], ea_s, ea_r.at[0], host_dev)
        all_sent(fsend, y_s, y_r.at[0, 0], host_dev)
    all_sent(rcore, rc_s, rc_r, core_dev)
    all_sent(idx.at[pl.ds(0, n - 1)], i_s, i_r.at[0], core_dev)
    all_sent(gat.at[pl.ds(0, nz * nx)], ac_s, gc_r.at[0], core_dev)
    if nx > 1:
        all_sent(xs, xs_s, xr_r.at[0], core_dev)
        all_sent(gat.at[pl.ds(0, nz * (nx - 1))], ax_s, gc_r.at[0], core_dev)
    if nz > 1:
        all_sent(chain.at[pl.ds(0, nz - 1)], ch_s, ci_r.at[0, 0], core_dev)
    for q in range(nz - 1):

        @pl.when(z == q)
        def _(q=q):
            all_sent(gat.at[pl.ds(0, q + 1)], azr_s, gc_r.at[0], core_dev)

        @pl.when(zr == q)
        def _(q=q):
            all_sent(gat.at[pl.ds(0, q + 1)], azl_s, gc_r.at[0], core_dev)

    pltpu.make_async_copy(new_weight, new_weight_o, w_s).wait()
    accum_out.wait()
    grad_out_copy.wait()
    for d in range(nh):
        k = lax.rem(h + d, nh)
        buf, acc = (ev_rows, ev_acc) if d == 0 else (rows_in, acc_in)
        for copy in held_out(buf, acc, k):
            copy.wait()


def write_kernel(*refs):
    sems = refs[10]
    copies = [pltpu.make_async_copy(refs[k], refs[5 + k], sems.at[k]) for k in range(5)]
    for copy in copies:
        copy.start()
    for copy in copies:
        copy.wait()


def on_device(
    nz, nx,
    pooled, w_up, grad_out, owners, rows, lookup_weight, lens, slot_map,
    cache_weight, cache_accum, evict_slots, evict_dest, evict_count,
):
    tables, batch, bag = owners.shape
    slots = slot_map.shape[-1]
    rows_dev = slots // tables
    emb = cache_weight.shape[-1]
    n = lax.axis_size("tbl")
    nh = lax.axis_size("hst")
    feat_n, hid = w_up.shape
    out_rows = feat_n // n
    width = tables * emb
    groups = slots // emb
    list_len = evict_slots.shape[-1]
    cap = list_len // 2
    cut = hid // CUTS
    tile = min(512, hid)

    dma = pltpu.SemaphoreType.DMA
    anyspace = pl.BlockSpec(memory_space=pltpu.HBM)
    i32 = jnp.int32
    grad_up, new_weight, new_accum, held_rows, held_accum = pl.pallas_call(
        functools.partial(step_kernel, nz, nx, nh, tables, rows_dev, tile),
        out_shape=(
            jax.ShapeDtypeStruct((out_rows, hid), F32),
            jax.ShapeDtypeStruct((slots, emb), F32),
            jax.ShapeDtypeStruct((groups, emb), F32),
            jax.ShapeDtypeStruct((nh, cap, emb), F32),
            jax.ShapeDtypeStruct((nh, 1, cap), F32),
        ),
        in_specs=[anyspace] * 12 + [pl.BlockSpec(memory_space=pltpu.SMEM)],
        out_specs=(pl.BlockSpec(memory_space=pl.ANY),) * 5,
        scratch_shapes=[
            pltpu.VMEM((out_rows, hid), F32),
            pltpu.VMEM((slots, emb), F32),
            pltpu.VMEM((groups, emb), F32),
            pltpu.VMEM((batch, feat_n), BF16),
            pltpu.VMEM((feat_n, batch), BF16),
            pltpu.VMEM((feat_n, hid), BF16),
            pltpu.VMEM((batch, hid), BF16),
            pltpu.VMEM((batch, hid), BF16),
            pltpu.VMEM((tables, bag, batch), i32),
            pltpu.VMEM((tables, bag, batch), i32),
            pltpu.VMEM((tables, bag, batch), BF16),
            pltpu.VMEM((tables, batch), i32),
            pltpu.VMEM((1, slots), i32),
            pltpu.VMEM((slots, emb), F32),
            pltpu.VMEM((groups, emb), F32),
            pltpu.VMEM((1, list_len), i32),
            pltpu.VMEM((1, list_len), i32),
            pltpu.VMEM((batch, width), F32),
            pltpu.VMEM((nh - 1, batch, width), BF16),
            pltpu.VMEM((nh, batch, width), BF16),
            pltpu.VMEM((n, batch, width), BF16),
            pltpu.VMEM((n, tables, batch), F32),
            pltpu.VMEM((n, tables, batch), F32),
            pltpu.VMEM((CUTS, nz, nx, 2, out_rows, cut), F32),
            pltpu.VMEM((CUTS, nz, nx, out_rows, cut), F32),
            pltpu.VMEM((nz, CUTS, nx, out_rows, cut), BF16),
            pltpu.VMEM((nz, CUTS, nx, out_rows, cut), BF16),
            pltpu.VMEM((nz, CUTS, nx, out_rows, cut), BF16),
            pltpu.VMEM((max(nx - 1, 1), CUTS, out_rows, cut), BF16),
            pltpu.VMEM((nx, CUTS, out_rows, cut), BF16),
            pltpu.VMEM((slots, emb), F32),
            pltpu.VMEM((slots, emb), F32),
            pltpu.VMEM((groups, emb), i32),
            pltpu.VMEM((nh, cap), i32),
            pltpu.VMEM((nh, cap), i32),
            pltpu.SMEM((groups, emb), i32),
            pltpu.SMEM((nh, cap), i32),
            pltpu.SMEM((nh, cap), i32),
            pltpu.VMEM((nh, cap, emb), F32),
            pltpu.VMEM((nh, cap, emb), F32),
            pltpu.VMEM((nh, cap, emb), F32),
            pltpu.VMEM((nh, cap, emb), F32),
            pltpu.VMEM((nh, 1, cap), F32),
            pltpu.VMEM((nh, cap, emb), F32),
            pltpu.VMEM((nh, 1, cap), F32),
            pltpu.VMEM((nh, cap, emb), BF16),
            pltpu.VMEM((nh, cap, emb), BF16),
            pltpu.VMEM((nh, cap, emb), F32),
            dma((2 * (hid // tile) + 2 * BLOCKS - 1 + 11,)), dma((3,)),
            dma, dma((max(nh - 1, 1), PIECES)), dma, dma((nz * nx,)),
            dma, dma, dma, dma, dma((nz * nx, PIECES)), dma((nz * nx + 2 * nx,)), dma, dma,
            dma, dma((nz + 1, CUTS)), dma, dma((max(nx - 1, 1),)),
            dma, dma((nh,)), dma, dma((nh,)), dma((2 + 2 * nh,)), dma,
        ],
        compiler_params=pltpu.CompilerParams(
            collective_id=0, has_side_effects=True, vmem_limit_bytes=48 * 1024 * 1024
        ),
        name="step",
    )(*[pltpu.with_memory_space_constraint(v, pltpu.HBM) for v in (
        pooled, w_up, grad_out,
        jnp.transpose(owners, (0, 2, 1)), jnp.transpose(rows, (0, 2, 1)),
        jnp.transpose(lookup_weight, (0, 2, 1)), lens, slot_map.reshape(1, slots),
        cache_weight.reshape(slots, emb), cache_accum.reshape(groups, emb),
        evict_slots.reshape(1, list_len), evict_dest.reshape(1, list_len),
    )], evict_count)
    outs = (grad_up, new_weight, new_accum, held_rows, held_accum)
    hbm = pl.BlockSpec(memory_space=pltpu.HBM)
    grad_up, new_weight, new_accum, held_rows, held_accum = pl.pallas_call(
        write_kernel,
        out_shape=tuple(jax.ShapeDtypeStruct(v.shape, v.dtype) for v in outs),
        in_specs=[pl.BlockSpec(memory_space=pl.ANY)] * 5,
        out_specs=(hbm,) * 5,
        scratch_shapes=[dma((5,))],
        compiler_params=pltpu.CompilerParams(vmem_limit_bytes=1024 * 1024),
        name="write",
    )(*outs)
    return (
        grad_up,
        new_weight[None, None],
        new_accum.reshape(1, 1, slots),
        held_rows[None, None],
        held_accum.reshape(1, 1, nh, cap),
    )


def solution(mesh):
    n, nh = mesh.shape["tbl"], mesh.shape["hst"]
    nx = nh if n % (2 * nh) == 0 else 1
    nz = n // (2 * nx)
    placed = (
        P("tbl", None),
        P(None, "hst"),
        P("tbl", "hst"),
        P("hst", "tbl", None),
        P("hst", "tbl", None),
        P("hst", "tbl", None),
        P("hst", "tbl"),
        P("tbl", "hst", None),
        P("tbl", "hst", None, None),
        P("tbl", "hst", None),
        P("tbl", "hst", None),
        P("tbl", "hst", None),
        P("tbl", "hst"),
    )
    return jax.shard_map(
        functools.partial(on_device, nz, nx),
        mesh=mesh,
        in_specs=placed,
        out_specs=(
            P("tbl", "hst"),
            P("tbl", "hst", None, None),
            P("tbl", "hst", None),
            P("tbl", "hst", None, None, None),
            P("tbl", "hst", None, None),
        ),
        check_vma=False,
    )
```

```python
import functools

import jax
import jax.numpy as jnp
from jax import lax
from jax.experimental import pallas as pl
from jax.experimental.pallas import tpu as pltpu
from jax.sharding import PartitionSpec as P

LEARN_RATE = 0.05
EPSILON = 1e-08
MESH = pl.DeviceIdType.MESH
BLOCKS = 2
SUBS = 2
PIECES = BLOCKS * SUBS
CUTS = 4
UPDATE_TILES = 8
RADIX = 256
ROW_STEP = 2048.0
WEIGHT_STEP = 512.0
F32 = jnp.float32
BF16 = jnp.bfloat16
NT_DIMS = (((1,), (1,)), ((), ()))


def iota(shape, axis):
    return lax.broadcasted_iota(jnp.int32, shape, axis)


def step_kernel(
    nz, nx, nh, tables, rows_dev, tile,
    pooled, w_up, grad_out, owners, rows, lookup_weight, lens, slot_map,
    weight, accum, evict_slots, evict_dest, evict_count,
    grad_up_o, new_weight_o, new_accum_o, held_rows_o, held_accum_o,
    grad_up, new_weight, new_accum, pooled_v, pooled_t, w_v, go_v, delta, own_v, row_v, lw_v, len_v, map_v, weight_v, accum_v,
    es_v, ed_v,
    fown, fsend, ybuf, gat, idx, idxb, grad, rcore, chain, rin, lin, xs, xr, place,
    wide, inv_v, src_v, ev_v, inv_s, src_s, ev_s, ev_w, ev_a, ev_g, ev_rows, ev_acc, rows_in, acc_in, ev_half, half_in, ev_ok,
    ld_s, sm_s, y_s, y_r, i_s, i_r, azr_s, azl_s, ax_s, ac_s, g_r, gc_r, rc_s, rc_r,
    ch_s, ci_r, xs_s, xr_r, er_s, er_r, ea_s, ea_r, out_s, w_s,
):
    n = nz * nx * 2
    me = lax.axis_index("tbl")
    h = lax.axis_index("hst")
    c = lax.rem(me, 2)
    zx = me // 2
    x = lax.rem(zx, nx)
    z = zx // nx
    other = 1 - c
    batch, hid = grad_out.shape
    feat_n = pooled.shape[1]
    width = ybuf.shape[-1]
    emb = width // tables
    bag = owners.shape[1]
    slots = weight.shape[0]
    list_len = evict_slots.shape[1]
    cap = ev_rows.shape[1]
    out_rows = grad.shape[4]
    cut = hid // CUTS
    piece = batch // PIECES
    block = batch // BLOCKS
    tiles = hid // tile

    def at(zi, xi, ci):
        return (zi * nx + xi) * 2 + ci

    def xof(d):
        return lax.rem(x + d, nx)

    def rcopy(src, dst, s, r, dev):
        return pltpu.make_async_remote_copy(
            src_ref=src, dst_ref=dst, send_sem=s, recv_sem=r,
            device_id=dev, device_id_type=MESH,
        )

    def cols(hh):
        return pl.ds(pl.multiple_of(hh * width, width), width)

    def span(k):
        return pl.ds(k * piece, piece)

    def spanb(k):
        return pl.ds(k * block, block)

    def cutcols(j):
        return pl.ds(j * cut, cut)

    def tilecols(j):
        return pl.ds(j * tile, tile)

    p_loads = [
        pltpu.make_async_copy(pooled.at[spanb(k)], pooled_v.at[spanb(k)], ld_s.at[k])
        for k in range(BLOCKS)
    ]
    base = BLOCKS
    w_loads = [
        pltpu.make_async_copy(w_up.at[:, tilecols(j)], w_v.at[:, tilecols(j)], ld_s.at[base + j])
        for j in range(tiles)
    ]
    base = base + tiles
    g_first = [
        pltpu.make_async_copy(
            grad_out.at[spanb(0), tilecols(j)], go_v.at[spanb(0), tilecols(j)], ld_s.at[base + j]
        )
        for j in range(tiles)
    ]
    base = base + tiles
    g_loads = [
        pltpu.make_async_copy(grad_out.at[spanb(k)], go_v.at[spanb(k)], ld_s.at[base + k - 1])
        for k in range(1, BLOCKS)
    ]
    base = base + BLOCKS - 1
    small = [
        pltpu.make_async_copy(src, dst, ld_s.at[base + k])
        for k, (src, dst) in enumerate((
            (owners, own_v), (rows, row_v), (lookup_weight, lw_v), (lens, len_v),
            (slot_map, map_v), (evict_slots, es_v), (evict_dest, ed_v),
            (accum, accum_v), (weight, weight_v),
        ))
    ]
    p_loads[0].start()
    w_loads[0].start()
    g_first[0].start()
    barrier = pltpu.get_barrier_semaphore()

    def greet(d, carry):
        pl.semaphore_signal(
            barrier, inc=1, device_id={"tbl": lax.rem(me + d, n)}, device_id_type=MESH
        )
        return carry

    lax.fori_loop(1, n, greet, 0)
    for d in range(1, nh):
        pl.semaphore_signal(
            barrier, inc=1, device_id={"hst": lax.rem(h + d, nh)}, device_id_type=MESH
        )
    for j in range(1, tiles):
        w_loads[j].start()
        g_first[j].start()
    for copy in p_loads[1:] + small + g_loads:
        copy.start()

    def y_copy(d, k):
        h2 = lax.rem(h + d, nh)
        return rcopy(
            fsend.at[d - 1, span(k)], ybuf.at[h, span(k)], y_s, y_r.at[nh - d - 1, k], {"hst": h2}
        )

    def y_arrival(d, k):
        h2 = lax.rem(h + d, nh)
        return rcopy(
            fsend.at[d - 1, span(k)], ybuf.at[h2, span(k)], y_s, y_r.at[d - 1, k],
            {"hst": h2},
        )

    def deltas(k):
        p_loads[k].wait()
        if k > 0:
            g_loads[k - 1].wait()
        for j in range(tiles):
            if k == 0:
                w_loads[j].wait()
                g_first[j].wait()
            cs = pl.ds(j * tile, tile)
            p = jnp.dot(pooled_v[spanb(k), :], w_v[:, cs], preferred_element_type=F32)
            s = jax.nn.sigmoid(p)
            g = go_v[spanb(k), cs].astype(F32)
            delta[spanb(k), cs] = (g * s * (1.0 + p * (1.0 - s))).astype(BF16)

    def feats_out(k):
        for d in range(1, nh):
            h2 = lax.rem(h + d, nh)
            part = lax.dot_general(
                delta[spanb(k), :], w_v[cols(h2), :], NT_DIMS, preferred_element_type=F32
            )
            fsend[d - 1, spanb(k)] = part.astype(BF16)
            if k == 0 and d == 1:
                pl.semaphore_wait(barrier, n - 1 + nh - 1)
            y_copy(d, k * SUBS).start()

    def feats_rest(k):
        for q in range(1, SUBS):
            for d in range(1, nh):
                y_copy(d, k * SUBS + q).start()

    def feats_own(k):
        fown[spanb(k), :] = lax.dot_general(
            delta[spanb(k), :], w_v[cols(h), :], NT_DIMS, preferred_element_type=F32
        )

    def i_copy(d):
        o = lax.rem(me + d, n)
        return rcopy(idx.at[o], idxb.at[me], i_s, i_r.at[zx], {"tbl": o})

    def i_arrival(first, count):
        ref = idxb.at[pl.ds(first, count)]
        return rcopy(ref, ref, i_s, i_r.at[first // 2], {"tbl": at(z, x, other)})


    def g_copy(slot, k, sem, dev):
        ref = gat.at[slot, span(k)]
        return rcopy(ref, ref, sem, g_r.at[slot // 2, k], {"tbl": dev})


    def right_copy(zi, k):
        return g_copy(at(zi, x, c), k, azr_s, at(z + 1, x, c))

    def left_copy(zi, k):
        return g_copy(at(zi, x, c), k, azl_s, at(z - 1, x, c))

    def x_copy(zi, d, k):
        return g_copy(at(zi, x, c), k, ax_s, at(z, xof(d), c))

    both = jnp.minimum(z, nz - 1 - z)

    def ring(e):
        dist = (e + 1) // 2
        near = jnp.where(lax.rem(e, 2) == 1, z - dist, z + dist)
        dist = e - both
        far = jnp.where(z - dist >= 0, z - dist, z + dist)
        return jnp.where(e <= 2 * both, near, far)

    def c_copy(zi, xi, k):
        ref = gat.at[at(zi, xi, c), span(k)]
        late = (zi == ring(nz - 1)) & (xi != x)
        spot = jnp.where(late, nz * nx + 2 * xi + k // (PIECES // 2), zi * nx + xi)
        return rcopy(ref, ref, ac_s, gc_r.at[spot], {"tbl": at(z, x, other)})

    def arrived(slot, k):
        g_copy(slot, k, ac_s, at(z, x, other)).wait_recv()

    def gather_start(k):
        total = fown[span(k), :]
        for d in range(1, nh):
            y_arrival(d, k).wait_recv()
            total = total + ybuf[lax.rem(h + d, nh), span(k)].astype(F32)
        gat[me, span(k)] = total.astype(BF16)

        @pl.when(z + 1 < nz)
        def _():
            right_copy(z, k).start()

        @pl.when(z >= 1)
        def _():
            left_copy(z, k).start()

        for d in range(1, nx):
            x_copy(z, d, k).start()
        c_copy(z, x, k).start()

    def core_copy(j):
        return rcopy(
            grad.at[j, :, :, other], rcore.at[j], rc_s, rc_r, {"tbl": at(z, x, other)}
        )

    def weight_grad(j):
        part = jnp.dot(pooled_t[...], delta[:, cutcols(j)], preferred_element_type=F32)
        grad[j] = part.reshape(nz, nx, 2, out_rows, cut)
        core_copy(j).start()

    deltas(0)
    feats_out(0)
    for copy in small:
        copy.wait()
    for t in range(tables):
        used = iota((bag, batch), 0) < len_v[t : t + 1, :]
        code = (row_v[t] + 1).astype(F32) * ROW_STEP + lw_v[t].astype(F32) * WEIGHT_STEP
        code = jnp.where(used, code, 0.0)
        for o in range(n):
            idx[o, t : t + 1, :] = jnp.sum(
                jnp.where(own_v[t] == o, code, 0.0), axis=0, keepdims=True
            )
    idxb[me] = idx[me]

    def i_start(d, carry):
        i_copy(d).start()
        return carry

    lax.fori_loop(1, n, i_start, 0)

    feats_own(0)
    feats_rest(0)
    deltas(1)
    feats_out(1)
    feats_rest(1)
    gather_start(0)
    feats_own(1)
    pooled_t[...] = pooled_v[...].T
    weight_grad(0)
    for k in range(1, PIECES):
        gather_start(k)
        weight_grad(k)

    place[...] = jnp.zeros_like(place)
    chunk = min(RADIX, rows_dev)

    def proc(*picked, rows_of=slice(0, batch)):
        codes = [idxb[slot][:, rows_of] for slot in picked]
        count = rows_of.stop - rows_of.start
        bags = [gat[slot, pl.ds(rows_of.start, count), :] for slot in picked]
        for t in range(tables):
            pairs = []
            for code, bag_rows in zip(codes, bags):
                code = code[t : t + 1, :]
                row1 = jnp.floor(code * (1.0 / ROW_STEP))
                wgt = ((code - row1 * ROW_STEP) * (1.0 / WEIGHT_STEP)).astype(BF16)
                pairs.append((row1 - 1.0, wgt, bag_rows[:, t * emb : (t + 1) * emb]))
            ids = iota((chunk, count), 0).astype(F32).astype(BF16)
            for r0 in range(0, rows_dev, chunk):
                total = None
                for row, wgt, part in pairs:
                    near = row - float(r0)
                    near = jnp.where((near >= 0.0) & (near < float(chunk)), near, -1.0)
                    mark = jnp.where(ids == near.astype(BF16), wgt, jnp.zeros((), BF16))
                    prod = jnp.dot(mark, part, preferred_element_type=F32)
                    total = prod if total is None else total + prod
                place[pl.ds(t * rows_dev + r0, chunk), :] += total

    eye = iota((emb, emb), 0) == iota((emb, emb), 1)
    groups = slots // emb

    inv_copy = pltpu.make_async_copy(inv_v, inv_s, sm_s.at[0])
    src_copy = pltpu.make_async_copy(src_v, src_s, sm_s.at[1])
    ev_copy = pltpu.make_async_copy(ev_v, ev_s, sm_s.at[2])

    def prepare_inverse():
        home = map_v[...].astype(F32)
        high = jnp.floor(home * (1.0 / emb))
        low = home - high * emb
        from_row = iota((1, slots), 1).astype(F32)
        from_high = jnp.floor(from_row * (1.0 / RADIX))
        from_low = from_row - from_high * RADIX
        in_group = iota((groups, slots), 0).astype(F32) == high
        left = jnp.concatenate(
            [jnp.where(in_group, from_high, 0.0), jnp.where(in_group, from_low, 0.0)], axis=0
        ).astype(BF16)
        right = jnp.where(iota((emb, slots), 0).astype(F32) == low, 1.0, 0.0).astype(BF16)
        found = lax.dot_general(left, right, NT_DIMS, preferred_element_type=F32)
        inv = (found[:groups] * RADIX + found[groups:]).astype(jnp.int32)
        inv_v[...] = jnp.clip(inv, 0, slots - 1)
        inv_copy.start()
        return found.astype(BF16)


    def prepare_wide():
        for i in range(groups):
            col = jnp.sum(jnp.where(eye, accum_v[i : i + 1, :], 0.0), axis=1, keepdims=True)
            wide[i * emb : (i + 1) * emb, :] = jnp.broadcast_to(col, (emb, emb))

    def prepare_evict(found):
        live = iota((1, list_len), 1) < evict_count[0, 0]
        lanes = 8 * -(-nh // 8)
        mine = jnp.where((iota((lanes, list_len), 0) == ed_v[...]) & live, 1.0, 0.0)
        before = jnp.where(iota((list_len, list_len), 0) < iota((list_len, list_len), 1), 1.0, 0.0)
        goal = jnp.dot(mine.astype(BF16), before.astype(BF16), preferred_element_type=F32)
        slot1 = es_v[...].astype(F32)
        slot_high = jnp.floor(slot1 * (1.0 / RADIX))
        slot_low = slot1 - slot_high * RADIX
        parts = jnp.where(iota((8, list_len), 0) == 0, slot_high, slot_low).astype(BF16)
        for d in range(nh):
            hot = jnp.where(
                iota((cap, list_len), 0).astype(F32) == goal[d : d + 1], mine[d : d + 1], 0.0
            )
            ev_ok[d] = jnp.broadcast_to(jnp.sum(hot, axis=1, keepdims=True), (cap, emb))
            hot = hot.astype(BF16)
            got = lax.dot_general(parts, hot, NT_DIMS, preferred_element_type=F32)
            src = (got[0:1] * RADIX + got[1:2]).astype(jnp.int32)
            src_v[d : d + 1, :] = jnp.clip(src, 0, slots - 1)
            from_slot = got[0:1] * RADIX + got[1:2]
            slot_group = jnp.floor(from_slot * (1.0 / emb))
            slot_lane = from_slot - slot_group * emb
            lane_hot = jnp.where(iota((emb, cap), 0).astype(F32) == slot_lane, 1.0, 0.0)
            taken = jnp.dot(found, lane_hot.astype(BF16), preferred_element_type=F32)
            in_slot_group = iota((groups, cap), 0).astype(F32) == slot_group
            row_high = jnp.sum(jnp.where(in_slot_group, taken[:groups], 0.0), axis=0, keepdims=True)
            row_low = jnp.sum(jnp.where(in_slot_group, taken[groups:], 0.0), axis=0, keepdims=True)
            ev_row = (row_high * RADIX + row_low).astype(jnp.int32)
            ev_v[d : d + 1, :] = jnp.clip(ev_row, 0, slots - 1)
        src_copy.start()
        ev_copy.start()


    def gathered(ref, index):
        return jnp.concatenate([ref[pl.ds(index(q), 1), :] for q in range(8)], axis=0)

    unroll = 64

    def each_evicted(body):
        def trip(i, carry):
            k = i // (cap // unroll)
            p = lax.rem(i, cap // unroll) * unroll
            for b in range(0, unroll, 8):
                body(k, p + b, pl.ds(pl.multiple_of(p + b, 8), 8))
            return carry

        lax.fori_loop(0, nh * cap // unroll, trip, 0)

    def prepare_fetch():
        def fetch(k, p, rows_p):
            ev_w[k, rows_p, :] = gathered(weight_v, lambda q: src_s[k, p + q])
            ev_a[k, rows_p, :] = gathered(wide, lambda q: src_s[k, p + q])

        each_evicted(fetch)

    def rin_copy(t, j):
        return rcopy(
            chain.at[t, j], rin.at[t, j], ch_s, ci_r.at[t, j], {"tbl": at(z + 1, x, c)}
        )

    def lin_copy(t, j):
        return rcopy(
            chain.at[t, j], lin.at[t, j], ch_s, ci_r.at[jnp.where(t == z - 1, nz, t), j],
            {"tbl": at(z - 1, x, c)},
        )

    def lin_arrival(t, j):
        return rcopy(
            chain.at[t, j], lin.at[t, j], ch_s, ci_r.at[jnp.where(t == z, nz, t), j],
            {"tbl": at(z - 1, x, c)},
        )

    def own_sum(t, j, xi):
        return grad[j, t, xi, c] + rcore[j, t, xi]

    def chain_step(t, j, buf, copy):
        for xi in range(nx):
            s = own_sum(t, j, xi)
            if buf is not None:
                s = s + buf[t, j, xi].astype(F32)
            chain[t, j, xi] = s.astype(BF16)
        copy(t, j).start()


    def chain_heads():
        rcopy(rcore, rcore, rc_s, rc_r, {"tbl": at(z, x, other)}).wait_recv()

        @pl.when(z == 0)
        def _():
            def body(i, carry):
                for j in range(CUTS):
                    chain_step(nz - 1 - i, j, None, rin_copy)
                return carry

            lax.fori_loop(0, nz - 1, body, 0)

        @pl.when(z == nz - 1)
        def _():
            def body(i, carry):
                for j in range(CUTS):
                    chain_step(i, j, None, lin_copy)
                return carry

            lax.fori_loop(0, nz - 1, body, 0)

    def xs_copy(d, j):
        x2 = xof(d)
        return rcopy(xs.at[d - 1, j], xr.at[x, j], xs_s, xr_r.at[nx - d - 1], {"tbl": at(z, x2, c)})

    def xs_arrival(d):
        x2 = xof(d)
        return rcopy(xs.at[d - 1], xr.at[x2], xs_s, xr_r.at[d - 1], {"tbl": at(z, x2, c)})

    def finish_cut(j):
        @pl.when(z >= 1)
        def _():
            rin_copy(z, j).wait_recv()
            for xi in range(nx):
                grad[j, z, xi, c] += rin[z, j, xi].astype(F32)

        @pl.when(z + 1 < nz)
        def _():
            lin_arrival(z, j).wait_recv()
            for xi in range(nx):
                grad[j, z, xi, c] += lin[z, j, xi].astype(F32)

        for d in range(1, nx):
            xs[d - 1, j] = own_sum(z, j, xof(d)).astype(BF16)
            xs_copy(d, j).start()

    def from_z(zi, k, open_end, onward):
        arrived(at(zi, x, c), k)

        @pl.when(open_end)
        def _():
            onward(zi, k).start()

        for dx in range(1, nx):
            x_copy(zi, dx, k).start()
        c_copy(zi, x, k).start()

    def from_x(i):
        head = i < PIECES
        i2 = i - PIECES
        paired = i2 < 2 * PIECES * both
        r = lax.rem(i2, 2 * PIECES)
        i3 = i2 - 2 * PIECES * both
        e = jnp.where(
            head, 0,
            jnp.where(
                paired, 1 + 2 * (i2 // (2 * PIECES)) + lax.rem(r, 2), 1 + 2 * both + i3 // PIECES
            ),
        )
        k = jnp.where(head, i, jnp.where(paired, r // 2, lax.rem(i3, PIECES)))
        zi = ring(e)
        for dx in range(1, nx):
            arrived(at(zi, xof(dx), c), k)
            c_copy(zi, xof(dx), k).start()

    def expect(zi, xi):
        mine = at(zi, xi, c)

        @pl.when(mine != me)
        def _():
            i_arrival(at(zi, xi, 0), 2).wait_recv()

        @pl.when(mine == me)
        def _():
            i_arrival(at(zi, xi, 0), 1).wait_recv()

        return mine

    def core_slot(zi, xi):
        slot = at(zi, xi, other)
        ref = gat.at[slot]
        rcopy(ref, ref, ac_s, gc_r.at[zi * nx + xi], {"tbl": at(z, x, other)}).wait_recv()
        return slot

    halves = [slice(0, batch // 2), slice(batch // 2, batch)]
    final = ring(nz - 1)

    def core_half(xi, q):
        slot = at(final, xi, other)
        ref = gat.at[slot, pl.ds(q * (batch // 2), batch // 2)]
        core = {"tbl": at(z, x, other)}
        rcopy(ref, ref, ac_s, gc_r.at[nz * nx + 2 * xi + q], core).wait_recv()
        return slot

    def pair_proc(zi, xi):
        mine = expect(zi, xi)
        proc(mine, core_slot(zi, xi))

    zr = nz - 1 - z

    def step_body(i, carry):
        j = i // PIECES + 1
        k = lax.rem(i, PIECES)
        s = j - 1

        @pl.when(z - j >= 0)
        def _():
            from_z(z - j, k, z + 1 < nz, right_copy)

        @pl.when(z + j < nz)
        def _():
            from_z(z + j, k, z >= 1, left_copy)

        from_x(i)

        @pl.when((s <= nz - 2) & (z >= 1) & (z <= s))
        def _():
            t = nz - 1 - s + z
            rin_copy(t, k).wait_recv()
            chain_step(t, k, rin, rin_copy)

        @pl.when((s <= nz - 2) & (zr >= 1) & (zr <= s))
        def _():
            t = s - zr
            lin_arrival(t, k).wait_recv()
            chain_step(t, k, lin, lin_copy)

        @pl.when((s == nz - 1) & (k < CUTS - 1))
        def _():
            finish_cut(k)

        @pl.when(i == 0)
        def _():
            found = prepare_inverse()
            prepare_wide()
            prepare_evict(found)

        @pl.when(i == 1)
        def _():
            chain_heads()

        @pl.when(i == 2 * PIECES - 1)
        def _():
            inv_copy.wait()
            src_copy.wait()
            ev_copy.wait()
            prepare_fetch()

        @pl.when(i == PIECES * nz - 2)
        def _():
            def one(dx, carry):
                xi = xof(dx)
                proc(expect(final, xi), core_half(xi, 0), rows_of=halves[0])
                return carry

            lax.fori_loop(1, nx, one, 0)

        side = lax.rem(k, 2) == 0
        near = k < 2
        end = s == nz - 1
        below = z - s
        line = jnp.where(side & ((below >= 0) | ~end) & (s >= 1), below, z + s)
        near = near & ((side & (s >= 1)) | (~side & ~end))
        on_line = near & (line >= 0) & (line < nz)
        zi = jnp.where(on_line, line, ring(jnp.maximum(s - 1, 0)))
        half_pair = (lax.rem(s, 2) == 0) & (s - 1 <= 2 * both)
        at_rim = jnp.where((below >= 0) | (z + s < nz), 1, 0)
        on_side = (k == jnp.where(end, at_rim, jnp.where(half_pair, 3, 2))) & (s >= 1)

        @pl.when(on_line | on_side)
        def _():
            def one(dx, carry):
                pair_proc(zi, xof(dx))
                return carry

            lax.fori_loop(jnp.where(on_line, 0, 1), jnp.where(on_line, 1, nx), one, 0)

        return carry

    lax.fori_loop(0, PIECES * nz, step_body, 0)
    if nx == 1:
        finish_cut(CUTS - 1)
    for dx in range(1, nx):
        if dx == 1:
            finish_cut(CUTS - 1)
        proc(at(final, xof(dx), c), core_half(xof(dx), 1), rows_of=halves[1])

    def ev_gather(k, p, rows_p):
        ev_g[k, rows_p, :] = gathered(place, lambda q: ev_s[k, p + q])

    each_evicted(ev_gather)

    def er_copy(d, slot):
        k = lax.rem(h + d, nh)
        return rcopy(ev_half.at[k], half_in.at[slot], er_s, er_r.at[slot], {"hst": k})

    def ea_copy(d, slot):
        k = lax.rem(h + d, nh)
        return rcopy(ev_acc.at[k], acc_in.at[slot], ea_s, ea_r.at[slot], {"hst": k})

    for d in range(1, nh + 1):
        k = lax.rem(h + d, nh)
        for r0 in range(0, cap, emb):
            span_k = pl.ds(r0, emb)
            g = ev_g[k, span_k]
            acc = ev_a[k, span_k] + jnp.mean(g * g, axis=1, keepdims=True)
            left = ev_w[k, span_k] - LEARN_RATE * g / (jnp.sqrt(acc) + EPSILON)
            used = ev_ok[k, span_k] > 0.5
            ev_rows[k, span_k] = jnp.where(used, left, 0.0)
            ev_acc[k, :, span_k] = jnp.sum(jnp.where(eye & used, acc, 0.0), axis=0, keepdims=True)
        if d < nh:
            ev_half[k] = ev_rows[k].astype(BF16)
            er_copy(d, h).start()
            ea_copy(d, h).start()

    def held_out(buf, acc, k):
        return (
            pltpu.make_async_copy(buf.at[k], held_rows_o.at[k], out_s.at[2 + k]),
            pltpu.make_async_copy(acc.at[k], held_accum_o.at[k], out_s.at[2 + nh + k]),
        )

    for copy in held_out(ev_rows, ev_acc, h):
        copy.start()

    batch_tiles = max(u for u in (1, 2, 4, UPDATE_TILES) if groups % u == 0)
    spread = batch_tiles * emb

    def weight_out(i):
        at_i = pl.ds(pl.multiple_of(i * spread, spread), spread)
        return pltpu.make_async_copy(new_weight.at[at_i], new_weight_o.at[at_i], w_s)

    def update(i2, carry):
        for u in range(batch_tiles):
            i = i2 * batch_tiles + u
            total = jnp.zeros((8, emb), F32)
            for b in range(emb // 8):
                rows_b = pl.ds(pl.multiple_of(i * emb + b * 8, 8), 8)
                g = gathered(place, lambda q: inv_s[i, b * 8 + q])
                acc = wide[rows_b, :] + jnp.mean(g * g, axis=1, keepdims=True)
                new_weight[rows_b, :] = weight_v[rows_b, :] - LEARN_RATE * g / (
                    jnp.sqrt(acc) + EPSILON
                )
                diag = iota((8, emb), 1) == iota((8, emb), 0) + b * 8
                total = total + jnp.where(diag, acc, 0.0)
            new_accum[pl.ds(i, 1), :] = jnp.sum(total, axis=0, keepdims=True)
        weight_out(i2).start()
        return carry

    lax.fori_loop(0, groups // batch_tiles, update, 0)
    accum_out = pltpu.make_async_copy(new_accum, new_accum_o, out_s.at[0])
    accum_out.start()

    for d in range(1, nx):
        xs_arrival(d).wait_recv()
    for j in range(CUTS):
        s = own_sum(z, j, x)
        for d in range(1, nx):
            s = s + xr[xof(d), j].astype(F32)
        grad_up[:, cutcols(j)] = s
    grad_out_copy = pltpu.make_async_copy(grad_up, grad_up_o, out_s.at[1])
    grad_out_copy.start()

    for d in range(1, nh):
        k = lax.rem(h + d, nh)
        er_copy(d, k).wait_recv()
        ea_copy(d, k).wait_recv()
        rows_in[k] = half_in[k].astype(F32)
        for copy in held_out(rows_in, acc_in, k):
            copy.start()

    def all_sent(ref, sem, recv, dev):
        rcopy(ref, ref, sem, recv, dev).wait_send()

    core_dev = {"tbl": at(z, x, other)}
    if nh > 1:
        host_dev = {"hst": lax.rem(h + 1, nh)}
        all_sent(ev_half.at[pl.ds(0, nh - 1)], er_s, er_r.at[0], host_dev)
        all_sent(ev_acc.at[pl.ds(0, nh - 1)], ea_s, ea_r.at[0], host_dev)
        all_sent(fsend, y_s, y_r.at[0, 0], host_dev)
    all_sent(rcore, rc_s, rc_r, core_dev)
    all_sent(idx.at[pl.ds(0, n - 1)], i_s, i_r.at[0], core_dev)
    all_sent(gat.at[pl.ds(0, nz * nx)], ac_s, gc_r.at[0], core_dev)
    if nx > 1:
        all_sent(xs, xs_s, xr_r.at[0], core_dev)
        all_sent(gat.at[pl.ds(0, nz * (nx - 1))], ax_s, gc_r.at[0], core_dev)
    if nz > 1:
        all_sent(chain.at[pl.ds(0, nz - 1)], ch_s, ci_r.at[0, 0], core_dev)
    for q in range(nz - 1):

        @pl.when(z == q)
        def _(q=q):
            all_sent(gat.at[pl.ds(0, q + 1)], azr_s, gc_r.at[0], core_dev)

        @pl.when(zr == q)
        def _(q=q):
            all_sent(gat.at[pl.ds(0, q + 1)], azl_s, gc_r.at[0], core_dev)

    pltpu.make_async_copy(new_weight, new_weight_o, w_s).wait()
    accum_out.wait()
    grad_out_copy.wait()
    for d in range(nh):
        k = lax.rem(h + d, nh)
        buf, acc = (ev_rows, ev_acc) if d == 0 else (rows_in, acc_in)
        for copy in held_out(buf, acc, k):
            copy.wait()


def write_kernel(*refs):
    sems = refs[10]
    copies = [pltpu.make_async_copy(refs[k], refs[5 + k], sems.at[k]) for k in range(5)]
    for copy in copies:
        copy.start()
    for copy in copies:
        copy.wait()


def on_device(
    nz, nx,
    pooled, w_up, grad_out, owners, rows, lookup_weight, lens, slot_map,
    cache_weight, cache_accum, evict_slots, evict_dest, evict_count,
):
    tables, batch, bag = owners.shape
    slots = slot_map.shape[-1]
    rows_dev = slots // tables
    emb = cache_weight.shape[-1]
    n = lax.axis_size("tbl")
    nh = lax.axis_size("hst")
    feat_n, hid = w_up.shape
    out_rows = feat_n // n
    width = tables * emb
    groups = slots // emb
    list_len = evict_slots.shape[-1]
    cap = list_len // 2
    cut = hid // CUTS
    tile = min(512, hid)

    dma = pltpu.SemaphoreType.DMA
    anyspace = pl.BlockSpec(memory_space=pltpu.HBM)
    i32 = jnp.int32
    grad_up, new_weight, new_accum, held_rows, held_accum = pl.pallas_call(
        functools.partial(step_kernel, nz, nx, nh, tables, rows_dev, tile),
        out_shape=(
            jax.ShapeDtypeStruct((out_rows, hid), F32),
            jax.ShapeDtypeStruct((slots, emb), F32),
            jax.ShapeDtypeStruct((groups, emb), F32),
            jax.ShapeDtypeStruct((nh, cap, emb), F32),
            jax.ShapeDtypeStruct((nh, 1, cap), F32),
        ),
        in_specs=[anyspace] * 12 + [pl.BlockSpec(memory_space=pltpu.SMEM)],
        out_specs=(pl.BlockSpec(memory_space=pl.ANY),) * 5,
        scratch_shapes=[
            pltpu.VMEM((out_rows, hid), F32),
            pltpu.VMEM((slots, emb), F32),
            pltpu.VMEM((groups, emb), F32),
            pltpu.VMEM((batch, feat_n), BF16),
            pltpu.VMEM((feat_n, batch), BF16),
            pltpu.VMEM((feat_n, hid), BF16),
            pltpu.VMEM((batch, hid), BF16),
            pltpu.VMEM((batch, hid), BF16),
            pltpu.VMEM((tables, bag, batch), i32),
            pltpu.VMEM((tables, bag, batch), i32),
            pltpu.VMEM((tables, bag, batch), BF16),
            pltpu.VMEM((tables, batch), i32),
            pltpu.VMEM((1, slots), i32),
            pltpu.VMEM((slots, emb), F32),
            pltpu.VMEM((groups, emb), F32),
            pltpu.VMEM((1, list_len), i32),
            pltpu.VMEM((1, list_len), i32),
            pltpu.VMEM((batch, width), F32),
            pltpu.VMEM((nh - 1, batch, width), BF16),
            pltpu.VMEM((nh, batch, width), BF16),
            pltpu.VMEM((n, batch, width), BF16),
            pltpu.VMEM((n, tables, batch), F32),
            pltpu.VMEM((n, tables, batch), F32),
            pltpu.VMEM((CUTS, nz, nx, 2, out_rows, cut), F32),
            pltpu.VMEM((CUTS, nz, nx, out_rows, cut), F32),
            pltpu.VMEM((nz, CUTS, nx, out_rows, cut), BF16),
            pltpu.VMEM((nz, CUTS, nx, out_rows, cut), BF16),
            pltpu.VMEM((nz, CUTS, nx, out_rows, cut), BF16),
            pltpu.VMEM((max(nx - 1, 1), CUTS, out_rows, cut), BF16),
            pltpu.VMEM((nx, CUTS, out_rows, cut), BF16),
            pltpu.VMEM((slots, emb), F32),
            pltpu.VMEM((slots, emb), F32),
            pltpu.VMEM((groups, emb), i32),
            pltpu.VMEM((nh, cap), i32),
            pltpu.VMEM((nh, cap), i32),
            pltpu.SMEM((groups, emb), i32),
            pltpu.SMEM((nh, cap), i32),
            pltpu.SMEM((nh, cap), i32),
            pltpu.VMEM((nh, cap, emb), F32),
            pltpu.VMEM((nh, cap, emb), F32),
            pltpu.VMEM((nh, cap, emb), F32),
            pltpu.VMEM((nh, cap, emb), F32),
            pltpu.VMEM((nh, 1, cap), F32),
            pltpu.VMEM((nh, cap, emb), F32),
            pltpu.VMEM((nh, 1, cap), F32),
            pltpu.VMEM((nh, cap, emb), BF16),
            pltpu.VMEM((nh, cap, emb), BF16),
            pltpu.VMEM((nh, cap, emb), F32),
            dma((2 * (hid // tile) + 2 * BLOCKS - 1 + 11,)), dma((3,)),
            dma, dma((max(nh - 1, 1), PIECES)), dma, dma((nz * nx,)),
            dma, dma, dma, dma, dma((nz * nx, PIECES)), dma((nz * nx + 2 * nx,)), dma, dma,
            dma, dma((nz + 1, CUTS)), dma, dma((max(nx - 1, 1),)),
            dma, dma((nh,)), dma, dma((nh,)), dma((2 + 2 * nh,)), dma,
        ],
        compiler_params=pltpu.CompilerParams(
            collective_id=0, has_side_effects=True, vmem_limit_bytes=48 * 1024 * 1024
        ),
        name="step",
    )(*[pltpu.with_memory_space_constraint(v, pltpu.HBM) for v in (
        pooled, w_up, grad_out,
        jnp.transpose(owners, (0, 2, 1)), jnp.transpose(rows, (0, 2, 1)),
        jnp.transpose(lookup_weight, (0, 2, 1)), lens, slot_map.reshape(1, slots),
        cache_weight.reshape(slots, emb), cache_accum.reshape(groups, emb),
        evict_slots.reshape(1, list_len), evict_dest.reshape(1, list_len),
    )], evict_count)
    outs = (grad_up, new_weight, new_accum, held_rows, held_accum)
    hbm = pl.BlockSpec(memory_space=pltpu.HBM)
    grad_up, new_weight, new_accum, held_rows, held_accum = pl.pallas_call(
        write_kernel,
        out_shape=tuple(jax.ShapeDtypeStruct(v.shape, v.dtype) for v in outs),
        in_specs=[pl.BlockSpec(memory_space=pl.ANY)] * 5,
        out_specs=(hbm,) * 5,
        scratch_shapes=[dma((5,))],
        compiler_params=pltpu.CompilerParams(vmem_limit_bytes=1024 * 1024),
        name="write",
    )(*outs)
    return (
        grad_up,
        new_weight[None, None],
        new_accum.reshape(1, 1, slots),
        held_rows[None, None],
        held_accum.reshape(1, 1, nh, cap),
    )


def solution(mesh):
    n, nh = mesh.shape["tbl"], mesh.shape["hst"]
    nx = nh if n % (2 * nh) == 0 else 1
    nz = n // (2 * nx)
    placed = (
        P("tbl", None),
        P(None, "hst"),
        P("tbl", "hst"),
        P("hst", "tbl", None),
        P("hst", "tbl", None),
        P("hst", "tbl", None),
        P("hst", "tbl"),
        P("tbl", "hst", None),
        P("tbl", "hst", None, None),
        P("tbl", "hst", None),
        P("tbl", "hst", None),
        P("tbl", "hst", None),
        P("tbl", "hst"),
    )
    return jax.shard_map(
        functools.partial(on_device, nz, nx),
        mesh=mesh,
        in_specs=placed,
        out_specs=(
            P("tbl", "hst"),
            P("tbl", "hst", None, None),
            P("tbl", "hst", None),
            P("tbl", "hst", None, None, None),
            P("tbl", "hst", None, None),
        ),
        check_vma=False,
    )
```
